32 devices in a mesh: dp: 8 (over z, y), tensor: 4 (over x, core).
Axes of the slice: x: 2, y: 2, z: 4, core: 2. Of those that a mesh axis runs over, the one named last changes fastest.
Arguments:
- inputs: bfloat16 [16384, 2048], P(('dp', 'tensor')), may hold values from -6 to 6
- lengths: int32 [8], P('dp'), may hold values from 128 to 2048, as said below
- ln1_gain: bfloat16 [2048], replicated, may hold values from 0.5 to 1.5
- ln1_bias: bfloat16 [2048], replicated, may hold values from -1 to 1
- ln2_gain: bfloat16 [2048], replicated, may hold values from 0.5 to 1.5
- ln2_bias: bfloat16 [2048], replicated, may hold values from -1 to 1
- w_qkv: bfloat16 [2048, 6144], P(None, 'tensor'), may hold values from -0.1875 to 0.1875
- b_qkv: bfloat16 [6144], P('tensor'), may hold values from -1 to 1
- w_dense: bfloat16 [2048, 2048], P('tensor'), may hold values from -0.5 to 0.5
- b_dense: bfloat16 [2048], replicated, may hold values from -1 to 1
- w_fc1: bfloat16 [2048, 8192], P(None, 'tensor'), may hold values from -0.125 to 0.125
- b_fc1: bfloat16 [8192], P('tensor'), may hold values from -1 to 1
- w_fc2: bfloat16 [8192, 2048], P('tensor'), may hold values from -0.09375 to 0.09375
- b_fc2: bfloat16 [2048], replicated, may hold values from -1 to 1
- out_grad: bfloat16 [16384, 2048], P(('dp', 'tensor')), may hold values from -6 to 6
Outputs:
- outputs: bfloat16 [16384, 2048], P(('dp', 'tensor'))
- in_grad: float32 [16384, 2048], P(('dp', 'tensor'))
- g_ln1_gain: float32 [2048], replicated
- g_ln1_bias: float32 [2048], replicated
- g_ln2_gain: float32 [2048], replicated
- g_ln2_bias: float32 [2048], replicated
- g_w_qkv: float32 [2048, 6144], P(None, 'tensor')
- g_b_qkv: float32 [6144], P('tensor')
- g_w_dense: float32 [2048, 2048], P('tensor')
- g_b_dense: float32 [2048], replicated
- g_w_fc1: float32 [2048, 8192], P(None, 'tensor')
- g_b_fc1: float32 [8192], P('tensor')
- g_w_fc2: float32 [8192, 2048], P('tensor')
- g_b_fc2: float32 [2048], replicated
The draws below stay inside these ranges and needn't reach their ends.
Inputs may be any that keep to these rules, and one draw needn't show every extreme that they name: `lengths`: tokens of a sequence at places from its length on are padding; at least one sequence has length exactly 2048 and one exactly 128.
All inputs are finite; a program needn't handle non-finite values.
Results may differ from the reference program's by a relative error of at most 0.014.
The reference program's roundings to bfloat16 on the way count: a program that leaves them out, or rounds other values in their place, can miss the bound.
Values may be sent and summed in bfloat16 or wider, within the bound.
No kernel may reach another device: no remote copies, remote signals or barrier semaphores. Data moves between devices by JAX's collectives and lax.ppermute only.
A program may use at most 320 MiB of HBM per device.

```python
from functools import partial
import jax
import jax.numpy as jnp
from jax import lax

D = 2048
HEADS = 16
HD = 128
ROT = 32
FF = 8192
SEQ = 2048
MIN_LEN = 128
NSEQ = 8
TOKENS = 16384


def draw_lengths(key, part):
    length_key, order_key = jax.random.split(jax.random.fold_in(key, 17))
    drawn = jax.random.randint(length_key, (NSEQ,), MIN_LEN, SEQ + 1)
    order = jax.random.permutation(order_key, NSEQ)
    drawn = drawn.at[order[0]].set(SEQ)
    drawn = drawn.at[order[1]].set(MIN_LEN)
    return drawn.astype(jnp.int32)


def block_levels(own_key, dims, cuts, least, high):
    loudness = 1.0
    for axis_at, parts in cuts:
        draws = jax.random.uniform(jax.random.fold_in(jax.random.fold_in(own_key, 6), axis_at), (parts,), jnp.float32, least / len(cuts), high / len(cuts))
        loudness = loudness * jnp.repeat(jnp.exp(draws), dims[axis_at] // parts).reshape((-1,) + (1,) * (len(dims) - 1 - axis_at))
    return loudness


def scatter_about(key, extent, scale, most, cuts=(), kind=jnp.bfloat16):
    values = jax.random.normal(key, extent, jnp.float32) * scale
    if len(cuts) > 0:
        values = block_levels(key, extent, cuts, -0.22, 0.18) * values
    return jnp.clip(values, min=-most, max=most).astype(kind)


def setup_inputs(seed: int = 0) -> dict:
    seeds = jax.random.split(jax.random.key(seed), 16)
    return {
        "inputs": scatter_about(seeds[0], (TOKENS, D), 1.0, 6.0, ((0, 32),)),
        "lengths": draw_lengths(jax.random.fold_in(seeds[15], 71), 0),
        "ln1_gain": jnp.clip(1.0 + 0.1 * jax.random.normal(seeds[2], (D,), jnp.float32), 0.5, 1.5).astype(jnp.bfloat16),
        "ln1_bias": scatter_about(seeds[3], (D,), 0.2, 1.0),
        "ln2_gain": jnp.clip(1.0 + 0.1 * jax.random.normal(seeds[4], (D,), jnp.float32), 0.5, 1.5).astype(jnp.bfloat16),
        "ln2_bias": scatter_about(seeds[5], (D,), 0.2, 1.0),
        "w_qkv": scatter_about(seeds[6], (D, 3 * D), (D // 2) ** -0.5, 0.1875, ((1, 4),)),
        "b_qkv": scatter_about(seeds[7], (3 * D,), 0.2, 1.0, ((0, 4),)),
        "w_dense": scatter_about(seeds[8], (D, D), (D // 16) ** -0.5, 0.5, ((0, 4),)),
        "b_dense": scatter_about(seeds[9], (D,), 0.2, 1.0),
        "w_fc1": scatter_about(seeds[10], (D, FF), D ** -0.5, 0.125, ((1, 4),)),
        "b_fc1": scatter_about(seeds[11], (FF,), 0.2, 1.0, ((0, 4),)),
        "w_fc2": scatter_about(seeds[12], (FF, D), (FF // 2) ** -0.5, 0.09375, ((0, 4),)),
        "b_fc2": scatter_about(seeds[13], (D,), 0.2, 1.0),
        "out_grad": scatter_about(seeds[14], (TOKENS, D), 1.0, 6.0, ((0, 32),)),
    }


@jax.custom_vjp
def low(v):
    return lax.optimization_barrier(v.astype(jnp.bfloat16)).astype(jnp.float32)

@jax.custom_vjp
def low_back(v):
    return v

def low_keep(v):
    return (low(v), None)

def low_pass(kept, grad):
    return (grad,)

def back_keep(v):
    return (v, None)

def back_low(kept, grad):
    return (low(grad),)
low.defvjp(low_keep, low_pass)
low_back.defvjp(back_keep, back_low)

def precise(left, right):
    return jnp.dot(left, right, precision=lax.Precision.HIGHEST, preferred_element_type=jnp.float32)

def layer_norm(values, gain_vec, offset):
    average = lax.optimization_barrier(jnp.mean(values, axis=-1, keepdims=True))
    centred = values - average
    spread = lax.optimization_barrier(jnp.mean(centred * centred, axis=-1, keepdims=True))
    return centred * lax.rsqrt(spread + 1e-05) * gain_vec + offset

def rotary_tables(positions):
    places = jnp.arange(positions, dtype=jnp.float32)
    halves = jnp.arange(ROT // 2, dtype=jnp.float32)
    inverse = 10000.0 ** (-2.0 * halves / ROT)
    angles = places[:, None] * inverse[None, :]
    angles = jnp.concatenate([angles, angles], axis=1)
    return (jnp.cos(angles), jnp.sin(angles))

def rotate(block_data, cos_table, sin_table):
    turned = block_data[..., :ROT]
    front_half = turned[..., :ROT // 2]
    back_half = turned[..., ROT // 2:]
    swapped = jnp.concatenate([-back_half, front_half], axis=-1)
    result = turned * cos_table[:, None, :] + swapped * sin_table[:, None, :]
    return jnp.concatenate([result, block_data[..., ROT:]], axis=-1)

def head_attention(queries, key_rows, value_rows, length):
    scores = low_back(precise(queries, key_rows.T))
    places = jnp.arange(SEQ)
    allowed = (places[None, :] <= places[:, None]) & (places[None, :] < length)
    masked = jnp.where(allowed, scores, -1e+30)
    highest = lax.optimization_barrier(jnp.max(masked, axis=1, keepdims=True))
    weights = jnp.exp(masked - highest)
    attn_probs = weights / lax.optimization_barrier(jnp.sum(weights, axis=1, keepdims=True))
    return precise(low(attn_probs), value_rows)

def sequence_layer(token_rows, length, parameters):
    ln1_gain, ln1_bias, ln2_gain, ln2_bias, w_qkv, b_qkv, w_dense, b_dense, w_fc1, b_fc1, w_fc2, b_fc2 = parameters
    normed_one = low(layer_norm(token_rows, ln1_gain, ln1_bias))
    normed_two = low(layer_norm(token_rows, ln2_gain, ln2_bias))
    packed = low_back(precise(normed_one, w_qkv) + b_qkv).reshape(SEQ, HEADS, 3, HD)
    cos_table, sin_table = rotary_tables(SEQ)
    queries = low(rotate(packed[:, :, 0], cos_table, sin_table) * HD ** (-0.5))
    key_rows = low(rotate(packed[:, :, 1], cos_table, sin_table))
    value_rows = low(packed[:, :, 2])
    attend = jax.checkpoint(partial(head_attention, length=length))
    context = lax.map(lambda element: attend(element[0], element[1], element[2]), (queries.transpose(1, 0, 2), key_rows.transpose(1, 0, 2), value_rows.transpose(1, 0, 2)))
    context = context.transpose(1, 0, 2).reshape(SEQ, D)
    validity = (jnp.arange(SEQ) < length).astype(jnp.float32)[:, None]
    context = low(low_back(context * validity))
    attention = precise(context, w_dense) + b_dense
    hidden = low_back(precise(normed_two, w_fc1) + b_fc1)
    active = low(jax.nn.gelu(hidden, approximate=False))
    return token_rows + attention + precise(active, w_fc2) + b_fc2

def reference(inputs, lengths, ln1_gain, ln1_bias, ln2_gain, ln2_bias, w_qkv, b_qkv, w_dense, b_dense, w_fc1, b_fc1, w_fc2, b_fc2, out_grad):
    parameters = tuple((member.astype(jnp.float32) for member in (ln1_gain, ln1_bias, ln2_gain, ln2_bias, w_qkv, b_qkv, w_dense, b_dense, w_fc1, b_fc1, w_fc2, b_fc2)))
    token_rows = inputs.astype(jnp.float32).reshape(NSEQ, SEQ, D)
    layer_step = jax.checkpoint(sequence_layer)

    def forward(all_rows, weights):
        return lax.map(lambda element: layer_step(element[0], element[1], weights), (all_rows, lengths))
    result, pullback = jax.vjp(forward, token_rows, parameters)
    row_grad, grads = pullback(out_grad.astype(jnp.float32).reshape(NSEQ, SEQ, D))
    return (result.reshape(TOKENS, D).astype(jnp.bfloat16), row_grad.reshape(TOKENS, D), grads[0], grads[1], grads[2], grads[3], grads[4], grads[5], grads[6], grads[7], grads[8], grads[9], grads[10], grads[11])
```

```python
from functools import partial

import jax
import jax.numpy as jnp
from jax import lax
from jax.experimental import pallas as pl
from jax.experimental.pallas import tpu as pltpu
from jax.sharding import PartitionSpec as P

HD = 128
ROT = 32
SEQ = 2048
BLOCK = 512
EPS = 1e-05
F32 = jnp.float32
BF16 = jnp.bfloat16


def dot_nn(left, right):
    return lax.dot_general(left, right, (((1,), (0,)), ((), ())), preferred_element_type=F32)


def dot_nt(left, right):
    return lax.dot_general(left, right, (((1,), (1,)), ((), ())), preferred_element_type=F32)


def dot_tn(left, right):
    return lax.dot_general(left, right, (((0,), (0,)), ((), ())), preferred_element_type=F32)


def rotary_tables():
    places = jnp.arange(SEQ, dtype=F32)
    lanes = jnp.arange(HD)
    inverse = 10000.0 ** (-2.0 * (lanes % (ROT // 2)).astype(F32) / ROT)
    angles = places[:, None] * inverse[None, :]
    cosines, sines = jnp.cos(angles), jnp.sin(angles)
    turned = (lanes < ROT)[None, :]
    front = (lanes < ROT // 2)[None, :]
    cos_table = jnp.where(turned, cosines, 1.0)
    low_table = jnp.where(front, -sines, 0.0)
    high_table = jnp.where(turned & ~front, sines, 0.0)
    return cos_table, low_table, high_table


def shifted_mix(rows, low_rows, high_rows):
    half = ROT // 2
    return pltpu.roll(rows, HD - half, 1) * low_rows + pltpu.roll(rows, half, 1) * high_rows


def diagonal(shape):
    return lax.broadcasted_iota(jnp.int32, shape, 0) <= lax.broadcasted_iota(jnp.int32, shape, 1)


def attend_kernel(
    length_ref, packed_ref, cos_ref, low_ref, high_ref, q_ref, k_ref, v_ref, ctx_ref, lse_ref, vt_ref
):
    length = length_ref[0]
    scale = HD ** (-0.5)
    for index in range(SEQ // BLOCK):
        rows = pl.ds(index * BLOCK, BLOCK)
        cos_rows, low_rows, high_rows = cos_ref[rows, :], low_ref[rows, :], high_ref[rows, :]
        raw_query = packed_ref[rows, 0:HD]
        raw_key = packed_ref[rows, HD : 2 * HD]
        value = packed_ref[rows, 2 * HD : 3 * HD]
        query = (raw_query * cos_rows + shifted_mix(raw_query, low_rows, high_rows)) * scale
        q_ref[rows, :] = query.astype(BF16)
        key = raw_key * cos_rows + shifted_mix(raw_key, low_rows, high_rows)
        k_ref[rows, :] = key.astype(BF16)
        v_ref[rows, :] = value.astype(BF16)
        vt_ref[:, rows] = jnp.transpose(value).astype(BF16)
    for index in range(SEQ // BLOCK):
        before = index * BLOCK
        rows = pl.ds(before, BLOCK)

        @pl.when(before < length)
        def _(before=before, rows=rows):
            query = q_ref[rows, :]
            near = jnp.where(diagonal((BLOCK, BLOCK)), dot_nt(k_ref[rows, :], query), -1e30)
            highest = jnp.max(near, axis=0, keepdims=True)
            if before:
                far = dot_nt(k_ref[0:before, :], query)
                highest = jnp.maximum(highest, jnp.max(far, axis=0, keepdims=True))
            near = jnp.exp(near - highest)
            totals = jnp.sum(near, axis=0, keepdims=True)
            if before:
                far = jnp.exp(far - highest)
                totals = totals + jnp.sum(far, axis=0, keepdims=True)
            inverse = 1.0 / totals
            turned = dot_nn(vt_ref[:, rows], (near * inverse).astype(BF16))
            if before:
                turned = turned + dot_nn(vt_ref[:, 0:before], (far * inverse).astype(BF16))
            context = jnp.transpose(turned)
            places = before + lax.broadcasted_iota(jnp.int32, (BLOCK, HD), 0)
            ctx_ref[rows, :] = jnp.where(places < length, context, 0.0).astype(BF16)
            lse_ref[0, :, rows] = highest + jnp.log(totals)

        @pl.when(before >= length)
        def _(rows=rows):
            ctx_ref[rows, :] = jnp.zeros((BLOCK, HD), BF16)
            lse_ref[0, :, rows] = jnp.zeros((1, BLOCK), F32)


def attend(packed, length, tables):
    heads = packed.shape[1] // (3 * HD)
    table_spec = pl.BlockSpec((SEQ, HD), lambda h, n: (0, 0), pipeline_mode=pl.Buffered(1))
    head_spec = pl.BlockSpec((SEQ, HD), lambda h, n: (0, h))
    rows = jax.ShapeDtypeStruct((SEQ, heads * HD), BF16)
    pairs = heads * SEQ * SEQ // 2
    return pl.pallas_call(
        attend_kernel,
        out_shape=(rows, rows, rows, rows, jax.ShapeDtypeStruct((heads, 1, SEQ), F32)),
        grid_spec=pltpu.PrefetchScalarGridSpec(
            num_scalar_prefetch=1,
            grid=(heads,),
            in_specs=[pl.BlockSpec((SEQ, 3 * HD), lambda h, n: (0, h))] + [table_spec] * 3,
            out_specs=[head_spec] * 4 + [pl.BlockSpec((1, 1, SEQ), lambda h, n: (h, 0, 0))],
            scratch_shapes=[pltpu.VMEM((HD, SEQ), BF16)],
        ),
        compiler_params=pltpu.CompilerParams(vmem_limit_bytes=56 << 20),
        cost_estimate=pl.CostEstimate(
            flops=4 * pairs * HD, transcendentals=pairs, bytes_accessed=heads * SEQ * HD * 20
        ),
        name="attend",
    )(length, packed, *tables)


def attend_back_kernel(
    length_ref,
    q_ref,
    k_ref,
    v_ref,
    grad_ref,
    lse_ref,
    cos_ref,
    low_ref,
    high_ref,
    out_ref,
    kt_ref,
    dk_ref,
    dv_ref,
):
    length = length_ref[0]
    scale = HD ** (-0.5)
    kt_ref[...] = jnp.transpose(k_ref[...].astype(F32)).astype(BF16)
    dk_ref[...] = jnp.zeros_like(dk_ref)
    dv_ref[...] = jnp.zeros_like(dv_ref)

    def unturn(rows, grad):
        return grad * cos_ref[rows, :] - shifted_mix(grad, low_ref[rows, :], high_ref[rows, :])

    for index in range(SEQ // BLOCK):
        before = index * BLOCK
        rows = pl.ds(before, BLOCK)

        @pl.when(before < length)
        def _(before=before, rows=rows):
            query = q_ref[rows, :]
            places = before + lax.broadcasted_iota(jnp.int32, (BLOCK, HD), 0)
            grad = jnp.where(places < length, grad_ref[rows, :].astype(F32), 0.0).astype(BF16)
            lse = lse_ref[0, :, rows]
            parts = [rows] + ([pl.ds(0, before)] if before else [])
            probs, grads = [], []
            for number, keys in enumerate(parts):
                scores = dot_nt(k_ref[keys, :], query)
                if number == 0:
                    scores = jnp.where(diagonal((BLOCK, BLOCK)), scores, -1e30)
                probs.append(jnp.exp(scores - lse))
                grads.append(dot_nt(v_ref[keys, :], grad))
            centre = sum(
                jnp.sum(prob * prob_grad, axis=0, keepdims=True)
                for prob, prob_grad in zip(probs, grads)
            )
            turned = jnp.zeros((HD, BLOCK), F32)
            for keys, prob, prob_grad in zip(parts, probs, grads):
                score_grad = (prob * (prob_grad - centre)).astype(BF16)
                dv_ref[keys, :] += dot_nn(prob.astype(BF16), grad)
                dk_ref[keys, :] += dot_nn(score_grad, query)
                turned = turned + dot_nn(kt_ref[:, keys], score_grad)
            out_ref[rows, 0:HD] = unturn(rows, jnp.transpose(turned) * scale).astype(BF16)

        @pl.when(before >= length)
        def _(rows=rows):
            out_ref[rows, 0:HD] = jnp.zeros((BLOCK, HD), BF16)

    for index in range(SEQ // BLOCK):
        rows = pl.ds(index * BLOCK, BLOCK)
        out_ref[rows, HD : 2 * HD] = unturn(rows, dk_ref[rows, :]).astype(BF16)
        out_ref[rows, 2 * HD : 3 * HD] = dv_ref[rows, :].astype(BF16)


def attend_back(queries, key_rows, value_rows, grad, lse, length, tables):
    heads = queries.shape[1] // HD
    table_spec = pl.BlockSpec((SEQ, HD), lambda h, n: (0, 0), pipeline_mode=pl.Buffered(1))
    head_spec = pl.BlockSpec((SEQ, HD), lambda h, n: (0, h))
    pairs = heads * SEQ * SEQ // 2
    return pl.pallas_call(
        attend_back_kernel,
        out_shape=jax.ShapeDtypeStruct((SEQ, heads * 3 * HD), BF16),
        grid_spec=pltpu.PrefetchScalarGridSpec(
            num_scalar_prefetch=1,
            grid=(heads,),
            in_specs=[head_spec] * 4
            + [pl.BlockSpec((1, 1, SEQ), lambda h, n: (h, 0, 0))]
            + [table_spec] * 3,
            out_specs=pl.BlockSpec((SEQ, 3 * HD), lambda h, n: (0, h)),
            scratch_shapes=[
                pltpu.VMEM((HD, SEQ), BF16),
                pltpu.VMEM((SEQ, HD), F32),
                pltpu.VMEM((SEQ, HD), F32),
            ],
        ),
        compiler_params=pltpu.CompilerParams(vmem_limit_bytes=56 << 20),
        cost_estimate=pl.CostEstimate(
            flops=10 * pairs * HD, transcendentals=pairs, bytes_accessed=heads * SEQ * HD * 14
        ),
        name="attend_back",
    )(length, queries, key_rows, value_rows, grad, lse, *tables)


def swap_tensor(values, bit):
    count = lax.axis_size("tensor")
    return lax.ppermute(values, "tensor", [(t, t ^ bit) for t in range(count)])


def gather_rows(block):
    if lax.axis_size("tensor") != 4:
        return lax.all_gather(block, "tensor", axis=0, tiled=True)
    place = lax.axis_index("tensor")
    far = swap_tensor(block, 2)
    mate = swap_tensor(block, 1)
    far_mate = swap_tensor(far, 1)
    rows = block.shape[0]
    whole = jnp.zeros((4 * rows, block.shape[1]), block.dtype)
    for bits, part in ((0, block), (1, mate), (2, far), (3, far_mate)):
        whole = lax.dynamic_update_slice_in_dim(whole, part, (place ^ bits) * rows, 0)
    return whole


def scatter_rows(partial_rows):
    if lax.axis_size("tensor") != 4:
        return lax.psum_scatter(
            partial_rows.astype(BF16), "tensor", scatter_dimension=0, tiled=True
        ).astype(F32)
    place = lax.axis_index("tensor")
    chip, core = place // 2, place % 2
    blocks = partial_rows.reshape(2, 2, -1, partial_rows.shape[1])
    kept = lax.dynamic_index_in_dim(blocks, core, 1, False).astype(F32)
    sent = lax.dynamic_index_in_dim(blocks, 1 - core, 1, False).astype(BF16)
    both = kept + swap_tensor(sent, 1).astype(F32)
    sent = lax.dynamic_index_in_dim(both, 1 - chip, 0, False).astype(BF16)
    kept = lax.dynamic_index_in_dim(both, chip, 0, False)
    return kept + swap_tensor(sent, 2).astype(F32)


def gelu_parts(hidden):
    below = 0.5 * (1.0 + lax.erf(hidden * (0.5**0.5)))
    density = jnp.exp(-0.5 * hidden * hidden) * ((2.0 * jnp.pi) ** (-0.5))
    return hidden * below, below + hidden * density


def shards(
    inputs,
    lengths,
    ln1_gain,
    ln1_bias,
    ln2_gain,
    ln2_bias,
    w_qkv,
    b_qkv,
    w_dense,
    b_dense,
    w_fc1,
    b_fc1,
    w_fc2,
    b_fc2,
    out_grad,
):
    own_rows, width = inputs.shape
    tables = rotary_tables()
    gain_one, gain_two = ln1_gain.astype(F32), ln2_gain.astype(F32)

    def centred(rows):
        rows = rows.astype(F32)
        middle = rows - jnp.mean(rows, axis=-1, keepdims=True)
        spread = jnp.mean(middle * middle, axis=-1, keepdims=True)
        rate = lax.rsqrt(spread + EPS)
        return middle * rate, rate

    whole_in = gather_rows(inputs)
    xhat, _ = centred(whole_in)
    whole_one = (xhat * gain_one + ln1_bias.astype(F32)).astype(BF16)
    whole_two = (xhat * gain_two + ln2_bias.astype(F32)).astype(BF16)
    grad_rows = gather_rows(out_grad)

    hidden = dot_nn(whole_two, w_fc1) + b_fc1.astype(F32)
    active, slope = gelu_parts(hidden)
    active = active.astype(BF16)
    fc2_grad = dot_tn(active, grad_rows).astype(BF16)
    fc2_sum = lax.psum(fc2_grad, "dp")
    hidden_grad = (dot_nt(grad_rows, w_fc2) * slope).astype(BF16)
    fc1_grad = dot_tn(whole_two, hidden_grad).astype(BF16)
    fc1_grad, fc2_sum = lax.optimization_barrier((fc1_grad, fc2_sum))
    fc1_sum = lax.psum(fc1_grad, "dp")
    fc1_bias_grad = jnp.sum(hidden_grad, axis=0, dtype=F32)

    whole_one, fc1_grad = lax.optimization_barrier((whole_one, fc1_grad))
    packed = dot_nn(whole_one, w_qkv) + b_qkv.astype(F32)
    queries, key_rows, value_rows, context, lse = attend(packed, lengths, tables)
    context_grad = dot_nt(grad_rows, w_dense).astype(BF16)
    packed_grad = attend_back(queries, key_rows, value_rows, context_grad, lse, lengths, tables)
    dense_grad = dot_tn(context, grad_rows).astype(BF16)
    qkv_grad = dot_tn(whole_one, packed_grad).astype(BF16)
    dense_grad, qkv_grad, fc1_sum = lax.optimization_barrier((dense_grad, qkv_grad, fc1_sum))
    dense_sum, qkv_sum = lax.psum((dense_grad, qkv_grad), "dp")
    qkv_bias_grad = jnp.sum(packed_grad, axis=0, dtype=F32)

    branches = scatter_rows(dot_nn(context, w_dense) + dot_nn(active, w_fc2))
    outputs = inputs.astype(F32) + branches + (b_dense.astype(F32) + b_fc2.astype(F32))

    normed_two = scatter_rows(dot_nt(hidden_grad, w_fc1))
    normed_one = scatter_rows(dot_nt(packed_grad, w_qkv))
    own_hat, rate = centred(inputs)
    own_grad = out_grad.astype(F32)

    def norm_back(grad, gain):
        scaled = grad * gain
        return rate * (
            scaled
            - jnp.mean(scaled, axis=-1, keepdims=True)
            - own_hat * jnp.mean(scaled * own_hat, axis=-1, keepdims=True)
        )

    in_grad = own_grad + norm_back(normed_one, gain_one) + norm_back(normed_two, gain_two)
    shared = jnp.stack(
        [
            jnp.sum(normed_one * own_hat, axis=0),
            jnp.sum(normed_one, axis=0),
            jnp.sum(normed_two * own_hat, axis=0),
            jnp.sum(normed_two, axis=0),
            jnp.sum(own_grad, axis=0),
        ]
    ).reshape(-1)
    sliced = jnp.concatenate([qkv_bias_grad, fc1_bias_grad])
    place = lax.axis_index("tensor")
    slots = jnp.zeros((lax.axis_size("tensor"), sliced.shape[0]), F32)
    slots = lax.dynamic_update_slice_in_dim(slots, sliced[None], place, 0)
    sums = lax.psum(jnp.concatenate([shared, slots.reshape(-1)]), ("dp", "tensor"))
    vectors = sums[: shared.shape[0]].reshape(5, width)
    slots = sums[shared.shape[0] :].reshape(slots.shape)
    own_slot = lax.dynamic_index_in_dim(slots, place, 0, False)
    return (
        outputs.astype(BF16),
        in_grad,
        vectors[0],
        vectors[1],
        vectors[2],
        vectors[3],
        qkv_sum.astype(F32),
        own_slot[: b_qkv.shape[0]],
        dense_sum.astype(F32),
        vectors[4],
        fc1_sum.astype(F32),
        own_slot[b_qkv.shape[0] :],
        fc2_sum.astype(F32),
        vectors[4],
    )


def solution(mesh):
    rows = P(("dp", "tensor"), None)
    columns = P(None, "tensor")
    inner = P("tensor", None)
    split = P("tensor")
    return jax.shard_map(
        shards,
        mesh=mesh,
        in_specs=(
            rows,
            P("dp"),
            P(),
            P(),
            P(),
            P(),
            columns,
            split,
            inner,
            P(),
            columns,
            split,
            inner,
            P(),
            rows,
        ),
        out_specs=(
            rows,
            rows,
            P(),
            P(),
            P(),
            P(),
            columns,
            split,
            inner,
            P(),
            columns,
            split,
            inner,
            P(),
        ),
        check_vma=False,
    )
```

```python
from functools import partial

import jax
import jax.numpy as jnp
from jax import lax
from jax.experimental import pallas as pl
from jax.experimental.pallas import tpu as pltpu
from jax.sharding import Mesh
from jax.sharding import PartitionSpec as P

HD = 128
ROT = 32
SEQ = 2048
BLOCK = 512
EPS = 1e-05
F32 = jnp.float32
BF16 = jnp.bfloat16


def dot_nn(left, right):
    return lax.dot_general(left, right, (((1,), (0,)), ((), ())), preferred_element_type=F32)


def dot_nt(left, right):
    return lax.dot_general(left, right, (((1,), (1,)), ((), ())), preferred_element_type=F32)


def dot_tn(left, right):
    return lax.dot_general(left, right, (((0,), (0,)), ((), ())), preferred_element_type=F32)


FORMS = {"nn": (1, 0), "nt": (1, 1), "tn": (0, 0)}


def matmul(form, pairs, kind, block, first=None, rows=None, extras=(), finish=None, chunk=None, name=None):
    sides = FORMS[form]
    height = pairs[0][0].shape[1 - sides[0]]
    rows = height if rows is None else rows
    block = min(block, rows)
    width = pairs[0][1].shape[1 - sides[1]]
    dims = (((sides[0],), (sides[1],)), ((), ()))
    count = len(pairs)
    chunk = width if chunk is None else min(chunk, width)

    def kernel(first_ref, *refs):
        for start in range(0, width, chunk):
            part = slice(start, start + chunk)
            rest = [ref[:, part] for ref in refs[2 * count : -1]]
            total = None
            for number in range(count):
                right = refs[2 * number + 1]
                product = lax.dot_general(
                    refs[2 * number][...],
                    right[part, :] if form == "nt" else right[:, part],
                    dims,
                    preferred_element_type=F32,
                )
                total = product if total is None else total + product
            if finish is not None:
                total = finish(total, *rest)
            refs[-1][:, part] = total.astype(kind)

    specs, flat = [], []
    for left, right in pairs:
        if form == "tn":
            specs.append(pl.BlockSpec((left.shape[0], block), lambda i, b: (0, b[0] + i)))
        else:
            specs.append(pl.BlockSpec((block, left.shape[1]), lambda i, b: (b[0] + i, 0)))
        specs.append(
            pl.BlockSpec(right.shape, lambda i, b: (0, 0), pipeline_mode=pl.Buffered(1))
        )
        flat.extend([left, right])
    for extra in extras:
        if extra.shape[0] == 1:
            specs.append(pl.BlockSpec(extra.shape, lambda i, b: (0, 0)))
        else:
            specs.append(pl.BlockSpec((block, width), lambda i, b: (b[0] + i, 0)))
        flat.append(extra)
    if first is None:
        first = jnp.zeros((), jnp.int32)
    inner = sum(left.shape[sides[0]] for left, _ in pairs)
    return pl.pallas_call(
        kernel,
        out_shape=jax.ShapeDtypeStruct((rows, width), kind),
        grid_spec=pltpu.PrefetchScalarGridSpec(
            num_scalar_prefetch=1,
            grid=(rows // block,),
            in_specs=specs,
            out_specs=pl.BlockSpec((block, width), lambda i, b: (i, 0)),
        ),
        compiler_params=pltpu.CompilerParams(vmem_limit_bytes=56 << 20),
        cost_estimate=pl.CostEstimate(
            flops=rows * width * inner // 8, transcendentals=0, bytes_accessed=rows * width
        ),
        name=name,
    )(first[None], *flat)


def rotary_tables():
    places = jnp.arange(SEQ, dtype=F32)
    lanes = jnp.arange(HD)
    inverse = 10000.0 ** (-2.0 * (lanes % (ROT // 2)).astype(F32) / ROT)
    angles = places[:, None] * inverse[None, :]
    cosines, sines = jnp.cos(angles), jnp.sin(angles)
    turned = (lanes < ROT)[None, :]
    front = (lanes < ROT // 2)[None, :]
    cos_table = jnp.where(turned, cosines, 1.0)
    low_table = jnp.where(front, -sines, 0.0)
    high_table = jnp.where(turned & ~front, sines, 0.0)
    return cos_table, low_table, high_table


def shifted_mix(rows, low_rows, high_rows):
    half = ROT // 2
    return pltpu.roll(rows, HD - half, 1) * low_rows + pltpu.roll(rows, half, 1) * high_rows


def diagonal(shape):
    return lax.broadcasted_iota(jnp.int32, shape, 0) <= lax.broadcasted_iota(jnp.int32, shape, 1)


def local_rows(index, place):
    return pl.ds(pl.multiple_of(lax.bitwise_xor(index, place) * BLOCK, BLOCK), BLOCK)


def attend_kernel(
    length_ref, packed_ref, cos_ref, low_ref, high_ref, q_ref, k_ref, v_ref, ctx_ref, lse_ref, vt_ref
):
    length, place = length_ref[0], length_ref[1]
    scale = HD ** (-0.5)
    for index in range(SEQ // BLOCK):
        rows = pl.ds(index * BLOCK, BLOCK)
        outside = local_rows(index, place)
        cos_rows, low_rows, high_rows = cos_ref[rows, :], low_ref[rows, :], high_ref[rows, :]
        raw_query = packed_ref[outside, 0:HD]
        raw_key = packed_ref[outside, HD : 2 * HD]
        value = packed_ref[outside, 2 * HD : 3 * HD]
        query = (raw_query * cos_rows + shifted_mix(raw_query, low_rows, high_rows)) * scale
        q_ref[rows, :] = query.astype(BF16)
        key = raw_key * cos_rows + shifted_mix(raw_key, low_rows, high_rows)
        k_ref[rows, :] = key.astype(BF16)
        v_ref[rows, :] = value.astype(BF16)
        vt_ref[:, rows] = jnp.transpose(value).astype(BF16)
    for index in range(SEQ // BLOCK):
        before = index * BLOCK
        rows = pl.ds(before, BLOCK)
        outside = local_rows(index, place)

        @pl.when(before < length)
        def _(before=before, rows=rows, outside=outside):
            query = q_ref[rows, :]
            near = jnp.where(diagonal((BLOCK, BLOCK)), dot_nt(k_ref[rows, :], query), -1e30)
            highest = jnp.max(near, axis=0, keepdims=True)
            if before:
                far = dot_nt(k_ref[0:before, :], query)
                highest = jnp.maximum(highest, jnp.max(far, axis=0, keepdims=True))
            near = jnp.exp(near - highest)
            totals = jnp.sum(near, axis=0, keepdims=True)
            if before:
                far = jnp.exp(far - highest)
                totals = totals + jnp.sum(far, axis=0, keepdims=True)
            inverse = 1.0 / totals
            turned = dot_nn(vt_ref[:, rows], (near * inverse).astype(BF16))
            if before:
                turned = turned + dot_nn(vt_ref[:, 0:before], (far * inverse).astype(BF16))
            context = jnp.transpose(turned)
            places = before + lax.broadcasted_iota(jnp.int32, (BLOCK, HD), 0)
            ctx_ref[outside, :] = jnp.where(places < length, context, 0.0).astype(BF16)
            lse_ref[0, :, rows] = highest + jnp.log(totals)

        @pl.when(before >= length)
        def _(rows=rows, outside=outside):
            ctx_ref[outside, :] = jnp.zeros((BLOCK, HD), BF16)
            lse_ref[0, :, rows] = jnp.zeros((1, BLOCK), F32)


def attend(packed, length, tables):
    heads = packed.shape[1] // (3 * HD)
    table_spec = pl.BlockSpec((SEQ, HD), lambda h, n: (0, 0), pipeline_mode=pl.Buffered(1))
    head_spec = pl.BlockSpec((SEQ, HD), lambda h, n: (0, h))
    rows = jax.ShapeDtypeStruct((SEQ, heads * HD), BF16)
    pairs = heads * SEQ * SEQ // 2
    return pl.pallas_call(
        attend_kernel,
        out_shape=(rows, rows, rows, rows, jax.ShapeDtypeStruct((heads, 1, SEQ), F32)),
        grid_spec=pltpu.PrefetchScalarGridSpec(
            num_scalar_prefetch=1,
            grid=(heads,),
            in_specs=[pl.BlockSpec((SEQ, 3 * HD), lambda h, n: (0, h))] + [table_spec] * 3,
            out_specs=[head_spec] * 4 + [pl.BlockSpec((1, 1, SEQ), lambda h, n: (h, 0, 0))],
            scratch_shapes=[pltpu.VMEM((HD, SEQ), BF16)],
        ),
        compiler_params=pltpu.CompilerParams(vmem_limit_bytes=56 << 20),
        cost_estimate=pl.CostEstimate(
            flops=4 * pairs * HD, transcendentals=pairs, bytes_accessed=heads * SEQ * HD * 20
        ),
        name="attend",
    )(length, packed, *tables)


def attend_back_kernel(
    length_ref,
    q_ref,
    k_ref,
    v_ref,
    grad_ref,
    lse_ref,
    cos_ref,
    low_ref,
    high_ref,
    out_ref,
    kt_ref,
    dk_ref,
    dv_ref,
):
    length, place = length_ref[0], length_ref[1]
    scale = HD ** (-0.5)
    kt_ref[...] = jnp.transpose(k_ref[...].astype(F32)).astype(BF16)
    dk_ref[...] = jnp.zeros_like(dk_ref)
    dv_ref[...] = jnp.zeros_like(dv_ref)

    def unturn(rows, grad):
        return grad * cos_ref[rows, :] - shifted_mix(grad, low_ref[rows, :], high_ref[rows, :])

    for index in range(SEQ // BLOCK):
        before = index * BLOCK
        rows = pl.ds(before, BLOCK)
        outside = local_rows(index, place)

        @pl.when(before < length)
        def _(before=before, rows=rows, outside=outside):
            query = q_ref[rows, :]
            places = before + lax.broadcasted_iota(jnp.int32, (BLOCK, HD), 0)
            grad = jnp.where(places < length, grad_ref[outside, :].astype(F32), 0.0).astype(BF16)
            lse = lse_ref[0, :, rows]
            parts = [rows] + ([pl.ds(0, before)] if before else [])
            probs, grads = [], []
            for number, keys in enumerate(parts):
                scores = dot_nt(k_ref[keys, :], query)
                if number == 0:
                    scores = jnp.where(diagonal((BLOCK, BLOCK)), scores, -1e30)
                probs.append(jnp.exp(scores - lse))
                grads.append(dot_nt(v_ref[keys, :], grad))
            centre = sum(
                jnp.sum(prob * prob_grad, axis=0, keepdims=True)
                for prob, prob_grad in zip(probs, grads)
            )
            turned = jnp.zeros((HD, BLOCK), F32)
            for keys, prob, prob_grad in zip(parts, probs, grads):
                score_grad = (prob * (prob_grad - centre)).astype(BF16)
                dv_ref[keys, :] += dot_nn(prob.astype(BF16), grad)
                dk_ref[keys, :] += dot_nn(score_grad, query)
                turned = turned + dot_nn(kt_ref[:, keys], score_grad)
            out_ref[outside, 0:HD] = unturn(rows, jnp.transpose(turned) * scale).astype(BF16)

        @pl.when(before >= length)
        def _(outside=outside):
            out_ref[outside, 0:HD] = jnp.zeros((BLOCK, HD), BF16)

    for index in range(SEQ // BLOCK):
        rows = pl.ds(index * BLOCK, BLOCK)
        outside = local_rows(index, place)
        out_ref[outside, HD : 2 * HD] = unturn(rows, dk_ref[rows, :]).astype(BF16)
        out_ref[outside, 2 * HD : 3 * HD] = dv_ref[rows, :].astype(BF16)


def attend_back(queries, key_rows, value_rows, grad, lse, length, tables):
    heads = queries.shape[1] // HD
    table_spec = pl.BlockSpec((SEQ, HD), lambda h, n: (0, 0), pipeline_mode=pl.Buffered(1))
    head_spec = pl.BlockSpec((SEQ, HD), lambda h, n: (0, h))
    pairs = heads * SEQ * SEQ // 2
    return pl.pallas_call(
        attend_back_kernel,
        out_shape=jax.ShapeDtypeStruct((SEQ, heads * 3 * HD), BF16),
        grid_spec=pltpu.PrefetchScalarGridSpec(
            num_scalar_prefetch=1,
            grid=(heads,),
            in_specs=[head_spec] * 4
            + [pl.BlockSpec((1, 1, SEQ), lambda h, n: (h, 0, 0))]
            + [table_spec] * 3,
            out_specs=pl.BlockSpec((SEQ, 3 * HD), lambda h, n: (0, h)),
            scratch_shapes=[
                pltpu.VMEM((HD, SEQ), BF16),
                pltpu.VMEM((SEQ, HD), F32),
                pltpu.VMEM((SEQ, HD), F32),
            ],
        ),
        compiler_params=pltpu.CompilerParams(vmem_limit_bytes=56 << 20),
        cost_estimate=pl.CostEstimate(
            flops=10 * pairs * HD, transcendentals=pairs, bytes_accessed=heads * SEQ * HD * 14
        ),
        name="attend_back",
    )(length, queries, key_rows, value_rows, grad, lse, *tables)


def hold(*values):
    return lax.optimization_barrier(values)


def swap_tensor(values, bit):
    count = lax.axis_size("tensor")
    return lax.ppermute(values, "tensor", [(t, t ^ bit) for t in range(count)])


def block_mask():
    return lax.axis_index("tensor") if lax.axis_size("tensor") == 4 else jnp.int32(0)


def gather_near(block):
    if lax.axis_size("tensor") != 4:
        return lax.all_gather(block, "tensor", axis=0, tiled=True), None
    return jnp.concatenate([block, swap_tensor(block, 1)]), swap_tensor(block, 2)


def gather_far(near, far):
    if far is None:
        return near
    return jnp.concatenate([near, far, swap_tensor(far, 1)])


def scatter_stages(partial_rows):
    if lax.axis_size("tensor") != 4:
        total = lax.psum_scatter(
            partial_rows.astype(BF16), "tensor", scatter_dimension=0, tiled=True
        )
        yield (total,)
        yield (total,)
        return total.astype(F32)
    own, mate, far, far_mate = jnp.split(partial_rows, 4)
    sent = jnp.concatenate([mate, far_mate]).astype(BF16)
    own, far, got = yield own.astype(F32), far.astype(F32), swap_tensor(sent, 1)
    rows = own.shape[0]
    own, far = own + got[:rows].astype(F32), far + got[rows:].astype(F32)
    own, got = yield own, swap_tensor(far.astype(BF16), 2)
    return own + got.astype(F32)


def add_rows(left, right):
    return (left.astype(F32) + right.astype(F32)).astype(left.dtype)


def move_z(values, pairs):
    return lax.ppermute(values, "z", pairs)


INWARD = ((0, 1), (3, 2))
MIDDLE = ((1, 2), (2, 1))
OUTWARD = ((1, 0), (2, 3))


def on_edge():
    z = lax.axis_index("z")
    return (z == 0) | (z == 3)


def sum_line(values):
    values = add_rows(values, move_z(values, INWARD))
    values = add_rows(values, move_z(values, MIDDLE))
    return jnp.where(on_edge(), move_z(values, OUTWARD), values)


PAIRS = ((0, 1), (1, 0))


def line_stages(kept, sent):
    if lax.axis_size("z") != 4:
        for _ in range(5):
            kept, sent = yield kept, sent
        return lax.psum(kept, ("z", "y")), lax.psum(sent, ("z", "y"))
    kept, got = yield kept, lax.ppermute(sent, "y", PAIRS)
    kept = add_rows(kept, got)
    kept, got = yield kept, move_z(kept, INWARD)
    kept = add_rows(kept, got)
    kept, got = yield kept, move_z(kept, MIDDLE)
    kept = add_rows(kept, got)
    kept, got = yield kept, move_z(kept, OUTWARD)
    kept = jnp.where(on_edge(), got, kept)
    kept, got = yield kept, lax.ppermute(kept, "y", PAIRS)
    return kept, got


def whole_rows(*pairs):
    own, other = [pair[0] for pair in pairs], [pair[1] for pair in pairs]
    upper = own_half()
    return jnp.concatenate(
        [jnp.where(upper == 0, x, y) for x, y in zip(own, other)]
        + [jnp.where(upper == 0, y, x) for x, y in zip(own, other)]
    ).astype(F32)


def own_half():
    return lax.axis_index("y") if lax.axis_size("z") == 4 else jnp.int32(0)


GATES = {
    "hidden_grad": "a",
    "fc1_grad": "",
    "packed_low": "b",
    "packed_high": "a",
    "attend_low": "",
    "attend_high": "c b",
    "dense_grad": "a",
    "back_low": "d c b",
    "qkv_low": "a e",
    "back_high": "d f c",
    "qkv_high": "b e",
    "to_two": "a c f d",
    "to_out": "e g n2",
    "to_one": "d b f o",
}
TAIL = (
    "e g",
    "n1 n2",
    "c",
    "f",
    "g",
    "o",
    "d",
    "g",
    "e",
    "n1",
    "f",
    "g",
)


class Piece:
    def __init__(self, stages):
        self.stages = stages
        self.waiting = next(stages)
        self.value = None

    def step(self, arrived):
        try:
            self.waiting = self.stages.send(arrived)
        except StopIteration as end:
            self.value, self.waiting = end.value, ()


def gate(pieces, *values):
    flat = list(values)
    for piece in pieces:
        flat.extend(piece.waiting)
    flat = hold(*flat)
    start = len(values)
    for piece in pieces:
        end = start + len(piece.waiting)
        piece.step(tuple(flat[start:end]))
        start = end
    flat = flat[: len(values)]
    moving = [piece for piece in pieces if len(piece.waiting) > 1]
    if moving and values:
        flat = list(hold(*flat, *[piece.waiting[0] for piece in moving]))
        for piece, kept in zip(moving, flat[len(values) :]):
            piece.waiting = (kept,) + piece.waiting[1:]
        flat = flat[: len(values)]
    return flat


def finish(*pieces):
    for piece in pieces:
        while piece.value is None:
            piece.step(piece.waiting)
    return [piece.value for piece in pieces]


def sum_small(values):
    if lax.axis_size("z") != 4 or lax.axis_size("tensor") != 4:
        return lax.psum(values, ("z", "y", "tensor"))
    values = values + swap_tensor(values, 1)
    values = values + swap_tensor(values, 2)
    values = values + lax.ppermute(values, "y", ((0, 1), (1, 0)))
    return sum_line(values)


def gelu_parts(hidden):
    below = 0.5 * (1.0 + lax.erf(hidden * (0.5**0.5)))
    density = jnp.exp(-0.5 * hidden * hidden) * ((2.0 * jnp.pi) ** (-0.5))
    return hidden * below, below + hidden * density


def shards(
    inputs,
    lengths,
    ln1_gain,
    ln1_bias,
    ln2_gain,
    ln2_bias,
    w_qkv,
    b_qkv,
    w_dense,
    b_dense,
    w_fc1,
    b_fc1,
    w_fc2,
    b_fc2,
    out_grad,
):
    own_rows, width = inputs.shape
    tables = rotary_tables()
    gain_one, gain_two = ln1_gain.astype(F32), ln2_gain.astype(F32)

    def centred(rows):
        rows = rows.astype(F32)
        middle = rows - jnp.mean(rows, axis=-1, keepdims=True)
        spread = jnp.mean(middle * middle, axis=-1, keepdims=True)
        rate = lax.rsqrt(spread + EPS)
        return middle * rate, rate

    scalars = jnp.stack([lengths[0], block_mask()])
    near_in, far_in = gather_near(inputs)
    near_out, far_out = gather_near(out_grad)
    xhat, _ = centred(gather_far(near_in, far_in))
    whole_one = (xhat * gain_one + ln1_bias.astype(F32)).astype(BF16)
    whole_two = (xhat * gain_two + ln2_bias.astype(F32)).astype(BF16)

    hidden = dot_nn(whole_two, w_fc1) + b_fc1.astype(F32)
    active = gelu_parts(hidden)[0].astype(BF16)
    if far_out is not None:
        near_out, far_out, active = hold(near_out, far_out, active)
    grad_rows = gather_far(near_out, far_out)
    upper = own_half()

    def half_gradient(left, right, side, number, parts):
        rows = left.shape[1] // 2 // parts
        part = lax.dynamic_slice_in_dim(left, (side * parts + number) * rows, rows, 1)
        return dot_tn(part, right).astype(BF16)

    def gradient(left, right, number, parts):
        sent = half_gradient(left, right, 1 - upper, number, parts)
        return hold(sent, left, right)

    def keep(left, right, number, parts):
        return half_gradient(left, right, upper, number, parts)

    token = scalars
    pieces = {}

    def at(place, *values):
        return gate([pieces[name] for name in GATES[place].split()], *values)

    sent_a, active, grad_rows = gradient(active, grad_rows, 0, 2)
    sent_b, active, grad_rows = gradient(active, grad_rows, 1, 2)
    kept_a = keep(active, grad_rows, 0, 2)
    kept_b = keep(active, grad_rows, 1, 2)
    pieces["a"] = Piece(line_stages(kept_a, sent_a))
    pieces["b"] = Piece(line_stages(kept_b, sent_b))
    grad_rows, kept_a, kept_b = hold(grad_rows, kept_a, kept_b)
    hidden_grad = matmul(
        "nt",
        [(grad_rows, w_fc2)],
        BF16,
        256,
        extras=[hidden],
        finish=lambda total, rows: total * gelu_parts(rows)[1],
        chunk=512,
        name="hidden_grad",
    )
    hidden_grad, whole_two = at("hidden_grad", hidden_grad, whole_two)
    fc1_bias_grad = jnp.sum(hidden_grad, axis=0, dtype=F32)
    sent_c, whole_two, hidden_grad = gradient(whole_two, hidden_grad, 0, 2)
    sent_d, whole_two, hidden_grad = gradient(whole_two, hidden_grad, 1, 2)
    kept_c = keep(whole_two, hidden_grad, 0, 2)
    kept_d = keep(whole_two, hidden_grad, 1, 2)
    pieces["c"] = Piece(line_stages(kept_c, sent_c))
    pieces["d"] = Piece(line_stages(kept_d, sent_d))
    kept_c, kept_d, whole_one = at("fc1_grad", kept_c, kept_d, whole_one)

    columns = w_qkv.shape[1] // 2

    def project(part, rows):
        return matmul(
            "nn",
            [(rows, w_qkv[:, part * columns : (part + 1) * columns])],
            F32,
            512,
            extras=[b_qkv[part * columns : (part + 1) * columns].astype(F32)[None]],
            finish=jnp.add,
            name="packed",
        )

    packed_low = project(0, whole_one)
    packed_low, whole_one = at("packed_low", packed_low, whole_one)
    packed_high = project(1, whole_one)
    packed_low, packed_high = at("packed_high", packed_low, packed_high)
    saved_low = attend(packed_low, scalars, tables)
    packed_high, *saved_low = at("attend_low", packed_high, *saved_low)
    saved_high = attend(packed_high, scalars, tables)
    context = jnp.concatenate([saved_low[3], saved_high[3]], axis=1)
    context, grad_rows = at("attend_high", context, grad_rows)
    sent_e, context, grad_rows = gradient(context, grad_rows, 0, 1)
    kept_e = keep(context, grad_rows, 0, 1)
    pieces["e"] = Piece(line_stages(kept_e, sent_e))
    inner = w_dense.shape[0] // 2
    grad_rows, kept_e = at("dense_grad", grad_rows, kept_e)

    def back(part, saved, rows):
        grad = dot_nt(rows, w_dense[part * inner : (part + 1) * inner]).astype(BF16)
        queries, key_rows, value_rows, _, lse = saved
        return attend_back(queries, key_rows, value_rows, grad, lse, scalars, tables)

    back_low = back(0, saved_low, grad_rows)
    back_low, grad_rows, whole_one = at("back_low", back_low, grad_rows, whole_one)
    sent_f, whole_one, back_low = gradient(whole_one, back_low, 0, 1)
    kept_f = keep(whole_one, back_low, 0, 1)
    pieces["f"] = Piece(line_stages(kept_f, sent_f))
    kept_f, grad_rows = at("qkv_low", kept_f, grad_rows)
    back_high = back(1, saved_high, grad_rows)
    back_high, whole_one = at("back_high", back_high, whole_one)
    sent_g, whole_one, back_high = gradient(whole_one, back_high, 0, 1)
    kept_g = keep(whole_one, back_high, 0, 1)
    pieces["g"] = Piece(line_stages(kept_g, sent_g))
    packed_grad = jnp.concatenate([back_low, back_high], axis=1)
    qkv_bias_grad = jnp.sum(packed_grad, axis=0, dtype=F32)
    hidden_grad, kept_g, packed_grad = at("qkv_high", hidden_grad, kept_g, packed_grad)
    to_two = matmul("nt", [(hidden_grad, w_fc1)], BF16, 512, name="to_two")
    pieces["n2"] = Piece(scatter_stages(to_two))
    to_two, context, active = at("to_two", to_two, context, active)
    to_out = matmul("nn", [(context, w_dense), (active, w_fc2)], BF16, 512, name="to_out")
    pieces["o"] = Piece(scatter_stages(to_out))
    to_out, packed_grad = at("to_out", to_out, packed_grad)
    to_one = matmul("nt", [(packed_grad, w_qkv)], BF16, 512, name="to_one")
    pieces["n1"] = Piece(scatter_stages(to_one))
    to_one, token = at("to_one", to_one, token)
    for names in TAIL:
        (token,) = gate([pieces[name] for name in names.split()], token)
    sums = finish(*[pieces[name] for name in ("a", "b", "c", "d", "e", "f", "g", "n1", "n2", "o")])
    fc2_sum, fc1_sum = whole_rows(*sums[0:2]), whole_rows(*sums[2:4])
    qkv_sum = jnp.concatenate([whole_rows(sums[5]), whole_rows(sums[6])], axis=1)
    sums[4] = whole_rows(sums[4])
    dense_sum, normed_one, normed_two, branches = sums[4], sums[7], sums[8], sums[9]
    outputs = inputs.astype(F32) + branches + (b_dense.astype(F32) + b_fc2.astype(F32))

    own_hat, rate = centred(inputs)
    own_grad = out_grad.astype(F32)

    def norm_back(grad, gain):
        scaled = grad * gain
        return rate * (
            scaled
            - jnp.mean(scaled, axis=-1, keepdims=True)
            - own_hat * jnp.mean(scaled * own_hat, axis=-1, keepdims=True)
        )

    in_grad = own_grad + norm_back(normed_one, gain_one) + norm_back(normed_two, gain_two)
    shared = jnp.stack(
        [
            jnp.sum(normed_one * own_hat, axis=0),
            jnp.sum(normed_one, axis=0),
            jnp.sum(normed_two * own_hat, axis=0),
            jnp.sum(normed_two, axis=0),
            jnp.sum(own_grad, axis=0),
        ]
    ).reshape(-1)
    sliced = jnp.concatenate([qkv_bias_grad, fc1_bias_grad])
    place = lax.axis_index("tensor")
    slots = jnp.zeros((lax.axis_size("tensor"), sliced.shape[0]), F32)
    slots = lax.dynamic_update_slice_in_dim(slots, sliced[None], place, 0)
    sums = sum_small(jnp.concatenate([shared, slots.reshape(-1)]).reshape(-1, HD)).reshape(-1)
    vectors = sums[: shared.shape[0]].reshape(5, width)
    slots = sums[shared.shape[0] :].reshape(slots.shape)
    own_slot = lax.dynamic_index_in_dim(slots, place, 0, False)
    return (
        outputs.astype(BF16),
        in_grad,
        vectors[0],
        vectors[1],
        vectors[2],
        vectors[3],
        qkv_sum,
        own_slot[: b_qkv.shape[0]],
        dense_sum,
        vectors[4],
        fc1_sum,
        own_slot[b_qkv.shape[0] :],
        fc2_sum,
        vectors[4],
    )


def solution(mesh):
    sequences, width = mesh.shape["dp"], mesh.shape["tensor"]
    mesh = Mesh(mesh.devices.reshape(sequences // 2, 2, width), ("z", "y", "tensor"))
    rows = P(("z", "y", "tensor"), None)
    columns = P(None, "tensor")
    inner = P("tensor", None)
    split = P("tensor")
    return jax.shard_map(
        shards,
        mesh=mesh,
        in_specs=(
            rows,
            P(("z", "y")),
            P(),
            P(),
            P(),
            P(),
            columns,
            split,
            inner,
            P(),
            columns,
            split,
            inner,
            P(),
            rows,
        ),
        out_specs=(
            rows,
            rows,
            P(),
            P(),
            P(),
            P(),
            columns,
            split,
            inner,
            P(),
            columns,
            split,
            inner,
            P(),
        ),
        check_vma=False,
    )
```

```python
from functools import partial

import jax
import jax.numpy as jnp
from jax import lax
from jax.experimental import pallas as pl
from jax.experimental.pallas import tpu as pltpu
from jax.sharding import Mesh
from jax.sharding import PartitionSpec as P

HD = 128
ROT = 32
SEQ = 2048
BLOCK = 512
EPS = 1e-05
HINT = 7
F32 = jnp.float32
BF16 = jnp.bfloat16


def dot_nn(left, right):
    return lax.dot_general(left, right, (((1,), (0,)), ((), ())), preferred_element_type=F32)


def dot_nt(left, right):
    return lax.dot_general(left, right, (((1,), (1,)), ((), ())), preferred_element_type=F32)


def dot_tn(left, right):
    return lax.dot_general(left, right, (((0,), (0,)), ((), ())), preferred_element_type=F32)


FORMS = {"nn": (1, 0), "nt": (1, 1)}


def matmul(form, pairs, kind, block, extras=(), finish=None, chunk=None, split=False, name=None):
    sides = FORMS[form]
    rows = pairs[0][0].shape[0]
    block = min(block, rows)
    pairs = [
        (left, right if isinstance(right, tuple) else (right, right.shape, (0, 0)))
        for left, right in pairs
    ]
    width = pairs[0][1][1][1 - sides[1]]
    dims = (((sides[0],), (sides[1],)), ((), ()))
    count = len(pairs)
    chunk = width if chunk is None else min(chunk, width)

    outs = 2 if split else 1

    def kernel(*refs):
        if split:
            for number in range(2):
                pl.when(pl.program_id(0) // 2 == number)(partial(fill, refs[:-2], refs[number - 2]))
        else:
            fill(refs[:-1], refs[-1])

    def fill(refs, out_ref):
        for start in range(0, width, chunk):
            part = slice(start, start + chunk)
            rest = [ref[:, part] for ref in refs[2 * count :]]
            total = None
            for number in range(count):
                right = refs[2 * number + 1]
                product = lax.dot_general(
                    refs[2 * number][...],
                    right[part, :] if form == "nt" else right[:, part],
                    dims,
                    preferred_element_type=F32,
                )
                total = product if total is None else total + product
            if finish is not None:
                total = finish(total, *rest)
            out_ref[:, part] = total.astype(kind)

    def at_row(i):
        return jnp.where(i < 2, 2 * i + 1, 2 * i - 4) if split else i

    specs, flat = [], []
    for left, (right, shape, index) in pairs:
        specs.append(pl.BlockSpec((block, left.shape[1]), lambda i: (at_row(i), 0)))
        specs.append(
            pl.BlockSpec(shape, lambda i, index=index: index, pipeline_mode=pl.Buffered(1))
        )
        flat.extend([left, right])
    for extra in extras:
        if isinstance(extra, tuple):
            extra, column = extra
            specs.append(pl.BlockSpec((block, width), lambda i, column=column: (i, column)))
        else:
            specs.append(pl.BlockSpec(extra.shape, lambda i: (0, 0)))
        flat.append(extra)
    inner = sum(left.shape[1] for left, _ in pairs)
    if split:
        out_specs = (
            pl.BlockSpec((block, width), lambda i: (jnp.minimum(i, 1), 0)),
            pl.BlockSpec((block, width), lambda i: (jnp.maximum(i - 2, 0), 0)),
        )
    else:
        out_specs = (pl.BlockSpec((block, width), lambda i: (i, 0)),)
    results = pl.pallas_call(
        kernel,
        out_shape=(jax.ShapeDtypeStruct((rows // outs, width), kind),) * outs,
        grid=(rows // block,),
        in_specs=specs,
        out_specs=out_specs,
        compiler_params=pltpu.CompilerParams(vmem_limit_bytes=56 << 20),
        cost_estimate=pl.CostEstimate(
            flops=rows * width * inner * HINT // 8, transcendentals=0, bytes_accessed=rows * width
        ),
        name=name,
    )(*flat)
    return results if split else results[0]


def gradient_kernel(upper_ref, left_ref, right_ref, sent_ref, kept_ref):
    product = lax.dot_general(
        left_ref[...], right_ref[...], (((0,), (0,)), ((), ())), preferred_element_type=F32
    ).astype(BF16)

    @pl.when(pl.program_id(0) == 0)
    def _():
        sent_ref[...] = product

    @pl.when(pl.program_id(0) == 1)
    def _():
        kept_ref[...] = product


def gradients(left, right, upper):
    height, width = left.shape[1] // 2, right.shape[1]
    block = min(512, height)
    steps = height // block
    shape = jax.ShapeDtypeStruct((height, width), BF16)
    return pl.pallas_call(
        gradient_kernel,
        out_shape=(shape, shape),
        grid_spec=pltpu.PrefetchScalarGridSpec(
            num_scalar_prefetch=1,
            grid=(2, steps),
            in_specs=[
                pl.BlockSpec(
                    (left.shape[0], block),
                    lambda s, i, u: (0, jnp.where(s == 0, 1 - u[0], u[0]) * steps + i),
                ),
                pl.BlockSpec(right.shape, lambda s, i, u: (0, 0), pipeline_mode=pl.Buffered(1)),
            ],
            out_specs=(
                pl.BlockSpec((block, width), lambda s, i, u: (jnp.where(s == 0, i, steps - 1), 0)),
                pl.BlockSpec((block, width), lambda s, i, u: (jnp.where(s == 0, 0, i), 0)),
            ),
        ),
        compiler_params=pltpu.CompilerParams(vmem_limit_bytes=48 << 20),
        cost_estimate=pl.CostEstimate(
            flops=2 * height * width * left.shape[0] * HINT // 8,
            transcendentals=0,
            bytes_accessed=height * width,
        ),
        name="gradients",
    )(upper[None], left, right)


def stack_kernel(*refs):
    for number in range(len(refs) - 1):

        @pl.when(pl.program_id(0) == number)
        def _(number=number):
            refs[-1][...] = refs[number][...]


def stack_rows(blocks):
    rows, width = blocks[0].shape
    return pl.pallas_call(
        stack_kernel,
        out_shape=jax.ShapeDtypeStruct((rows * len(blocks), width), blocks[0].dtype),
        grid=(len(blocks),),
        in_specs=[pl.BlockSpec((rows, width), lambda i: (0, 0))] * len(blocks),
        out_specs=pl.BlockSpec((rows, width), lambda i: (i, 0)),
        compiler_params=pltpu.CompilerParams(vmem_limit_bytes=32 << 20),
        name="stack_rows",
    )(*blocks)


def normalize_kernel(*refs, blocks):
    gains = [ref[...] for ref in refs[blocks : blocks + 4]]
    for number in range(blocks):

        @pl.when(pl.program_id(0) == number)
        def _(number=number):
            rows = refs[number][...].astype(F32)
            middle = rows - jnp.mean(rows, axis=-1, keepdims=True)
            spread = jnp.mean(middle * middle, axis=-1, keepdims=True)
            middle = middle * lax.rsqrt(spread + EPS)
            refs[-2][...] = (middle * gains[0] + gains[1]).astype(BF16)
            refs[-1][...] = (middle * gains[2] + gains[3]).astype(BF16)


def normalize(blocks, vectors, total, place, buffers=()):
    rows, width = blocks[0].shape
    step = min(256, rows)
    steps = rows // step
    count = len(blocks)

    def pick(number):
        return lambda s, i: (
            jnp.where(s == number, i, jnp.where(s < number, 0, steps - 1)),
            0,
        )

    shape = jax.ShapeDtypeStruct((total, width), BF16)
    out_spec = pl.BlockSpec((step, width), lambda s, i: ((place * count + s) * steps + i, 0))
    return pl.pallas_call(
        partial(normalize_kernel, blocks=count),
        out_shape=(shape, shape),
        grid=(count, steps),
        in_specs=[pl.BlockSpec((step, width), pick(number)) for number in range(count)]
        + [pl.BlockSpec((1, width), lambda s, i: (0, 0))] * 4
        + [pl.BlockSpec(memory_space=pl.ANY)] * len(buffers),
        out_specs=(out_spec, out_spec),
        input_output_aliases={count + 4 + n: n for n in range(len(buffers))},
        compiler_params=pltpu.CompilerParams(vmem_limit_bytes=40 << 20),
        name="normalize",
    )(*blocks, *vectors, *buffers)


def feed_forward_kernel(rows_ref, weight_ref, bias_ref, *refs, chunk):
    hidden_ref, active_ref = refs[-2:]
    for start in range(0, weight_ref.shape[1], chunk):
        part = slice(start, start + chunk)
        hidden = dot_nn(rows_ref[...], weight_ref[:, part]) + bias_ref[:, part]
        hidden_ref[:, part] = hidden
        active_ref[:, part] = gelu_parts(hidden)[0].astype(BF16)


def feed_forward(rows_in, weight, bias, place, parts, buffers=()):
    total, width = rows_in.shape
    wide = weight.shape[1]
    step = min(256, total)
    steps = total // step // parts
    out_spec = pl.BlockSpec((step, wide), lambda i: (place * steps + i, 0))
    return pl.pallas_call(
        partial(feed_forward_kernel, chunk=min(512, wide)),
        out_shape=(
            jax.ShapeDtypeStruct((total, wide), F32),
            jax.ShapeDtypeStruct((total, wide), BF16),
        ),
        grid=(steps,),
        in_specs=[
            pl.BlockSpec((step, width), lambda i: (place * steps + i, 0)),
            pl.BlockSpec(weight.shape, lambda i: (0, 0), pipeline_mode=pl.Buffered(1)),
            pl.BlockSpec((1, wide), lambda i: (0, 0)),
        ]
        + [pl.BlockSpec(memory_space=pl.ANY)] * len(buffers),
        out_specs=(out_spec, out_spec),
        input_output_aliases={3 + n: n for n in range(len(buffers))},
        compiler_params=pltpu.CompilerParams(vmem_limit_bytes=56 << 20),
        name="feed_forward",
    )(rows_in, weight, bias, *buffers)


def assemble_kernel(upper_ref, kept_ref, got_ref, *refs):
    @pl.when(pl.program_id(0) == 0)
    def _():
        refs[-1][...] = kept_ref[...].astype(F32)

    @pl.when(pl.program_id(0) == 1)
    def _():
        refs[-1][...] = got_ref[...].astype(F32)


def assemble(pair, upper, column, columns, buffer=None):
    kept, got = pair
    rows, width = kept.shape
    step = min(256, rows)
    steps = rows // step
    buffers = () if buffer is None else (buffer,)
    return pl.pallas_call(
        assemble_kernel,
        out_shape=jax.ShapeDtypeStruct((2 * rows, width * columns), F32),
        grid_spec=pltpu.PrefetchScalarGridSpec(
            num_scalar_prefetch=1,
            grid=(2, steps),
            in_specs=[
                pl.BlockSpec((step, width), lambda s, i, u: (jnp.where(s == 0, i, steps - 1), 0)),
                pl.BlockSpec((step, width), lambda s, i, u: (jnp.where(s == 0, 0, i), 0)),
            ]
            + [pl.BlockSpec(memory_space=pl.ANY)] * len(buffers),
            out_specs=pl.BlockSpec(
                (step, width),
                lambda s, i, u: (jnp.where(s == 0, u[0], 1 - u[0]) * steps + i, column),
            ),
        ),
        input_output_aliases={3: 0} if buffers else {},
        compiler_params=pltpu.CompilerParams(vmem_limit_bytes=24 << 20),
        name="assemble",
    )(upper[None], kept, got, *buffers)


def rotary_tables():
    places = jnp.arange(SEQ, dtype=F32)
    lanes = jnp.arange(HD)
    inverse = 10000.0 ** (-2.0 * (lanes % (ROT // 2)).astype(F32) / ROT)
    angles = places[:, None] * inverse[None, :]
    cosines, sines = jnp.cos(angles), jnp.sin(angles)
    turned = (lanes < ROT)[None, :]
    front = (lanes < ROT // 2)[None, :]
    cos_table = jnp.where(turned, cosines, 1.0)
    low_table = jnp.where(front, -sines, 0.0)
    high_table = jnp.where(turned & ~front, sines, 0.0)
    return cos_table, low_table, high_table


def shifted_mix(rows, low_rows, high_rows):
    half = ROT // 2
    return pltpu.roll(rows, HD - half, 1) * low_rows + pltpu.roll(rows, half, 1) * high_rows


def diagonal(shape):
    return lax.broadcasted_iota(jnp.int32, shape, 0) <= lax.broadcasted_iota(jnp.int32, shape, 1)


def local_rows(index, place):
    return pl.ds(pl.multiple_of(lax.bitwise_xor(index, place) * BLOCK, BLOCK), BLOCK)


def attend_kernel(
    length_ref, packed_ref, cos_ref, low_ref, high_ref, q_ref, k_ref, v_ref, ctx_ref, lse_ref, vt_ref
):
    length, place = length_ref[0], length_ref[1]
    scale = HD ** (-0.5)
    for index in range(SEQ // BLOCK):
        rows = pl.ds(index * BLOCK, BLOCK)
        outside = local_rows(index, place)
        cos_rows, low_rows, high_rows = cos_ref[rows, :], low_ref[rows, :], high_ref[rows, :]
        raw_query = packed_ref[outside, 0:HD]
        raw_key = packed_ref[outside, HD : 2 * HD]
        value = packed_ref[outside, 2 * HD : 3 * HD]
        query = (raw_query * cos_rows + shifted_mix(raw_query, low_rows, high_rows)) * scale
        q_ref[rows, :] = query.astype(BF16)
        key = raw_key * cos_rows + shifted_mix(raw_key, low_rows, high_rows)
        k_ref[rows, :] = key.astype(BF16)
        v_ref[rows, :] = value.astype(BF16)
        vt_ref[:, rows] = jnp.transpose(value).astype(BF16)
    for index in range(SEQ // BLOCK):
        before = index * BLOCK
        rows = pl.ds(before, BLOCK)
        outside = local_rows(index, place)

        @pl.when(before < length)
        def _(before=before, rows=rows, outside=outside):
            query = q_ref[rows, :]
            near = jnp.where(diagonal((BLOCK, BLOCK)), dot_nt(k_ref[rows, :], query), -1e30)
            highest = jnp.max(near, axis=0, keepdims=True)
            if before:
                far = dot_nt(k_ref[0:before, :], query)
                highest = jnp.maximum(highest, jnp.max(far, axis=0, keepdims=True))
            near = jnp.exp(near - highest)
            totals = jnp.sum(near, axis=0, keepdims=True)
            if before:
                far = jnp.exp(far - highest)
                totals = totals + jnp.sum(far, axis=0, keepdims=True)
            inverse = 1.0 / totals
            turned = dot_nn(vt_ref[:, rows], (near * inverse).astype(BF16))
            if before:
                turned = turned + dot_nn(vt_ref[:, 0:before], (far * inverse).astype(BF16))
            context = jnp.transpose(turned)
            places = before + lax.broadcasted_iota(jnp.int32, (BLOCK, HD), 0)
            ctx_ref[outside, :] = jnp.where(places < length, context, 0.0).astype(BF16)
            lse_ref[0, :, rows] = highest + jnp.log(totals)

        @pl.when(before >= length)
        def _(rows=rows, outside=outside):
            ctx_ref[outside, :] = jnp.zeros((BLOCK, HD), BF16)
            lse_ref[0, :, rows] = jnp.zeros((1, BLOCK), F32)


def attend(packed, length, tables):
    heads = packed.shape[1] // (3 * HD)
    table_spec = pl.BlockSpec((SEQ, HD), lambda h, n: (0, 0), pipeline_mode=pl.Buffered(1))
    head_spec = pl.BlockSpec((SEQ, HD), lambda h, n: (0, h))
    rows = jax.ShapeDtypeStruct((SEQ, heads * HD), BF16)
    pairs = heads * SEQ * SEQ // 2
    return pl.pallas_call(
        attend_kernel,
        out_shape=(rows, rows, rows, rows, jax.ShapeDtypeStruct((heads, 1, SEQ), F32)),
        grid_spec=pltpu.PrefetchScalarGridSpec(
            num_scalar_prefetch=1,
            grid=(heads,),
            in_specs=[pl.BlockSpec((SEQ, 3 * HD), lambda h, n: (0, h))] + [table_spec] * 3,
            out_specs=[head_spec] * 4 + [pl.BlockSpec((1, 1, SEQ), lambda h, n: (h, 0, 0))],
            scratch_shapes=[pltpu.VMEM((HD, SEQ), BF16)],
        ),
        compiler_params=pltpu.CompilerParams(vmem_limit_bytes=56 << 20),
        cost_estimate=pl.CostEstimate(
            flops=240 * HINT * pairs, transcendentals=0, bytes_accessed=heads * SEQ * HD * 20
        ),
        name="attend",
    )(length, packed, *tables)


def attend_back_kernel(
    length_ref,
    q_ref,
    k_ref,
    v_ref,
    grad_ref,
    lse_ref,
    cos_ref,
    low_ref,
    high_ref,
    out_ref,
    kt_ref,
    dk_ref,
    dv_ref,
):
    length, place = length_ref[0], length_ref[1]
    scale = HD ** (-0.5)
    kt_ref[...] = jnp.transpose(k_ref[...].astype(F32)).astype(BF16)
    dk_ref[...] = jnp.zeros_like(dk_ref)
    dv_ref[...] = jnp.zeros_like(dv_ref)

    def unturn(rows, grad):
        return grad * cos_ref[rows, :] - shifted_mix(grad, low_ref[rows, :], high_ref[rows, :])

    for index in range(SEQ // BLOCK):
        before = index * BLOCK
        rows = pl.ds(before, BLOCK)
        outside = local_rows(index, place)

        @pl.when(before < length)
        def _(before=before, rows=rows, outside=outside):
            query = q_ref[rows, :]
            places = before + lax.broadcasted_iota(jnp.int32, (BLOCK, HD), 0)
            grad = jnp.where(places < length, grad_ref[outside, :].astype(F32), 0.0).astype(BF16)
            lse = lse_ref[0, :, rows]
            parts = [rows] + ([pl.ds(0, before)] if before else [])
            probs, grads = [], []
            for number, keys in enumerate(parts):
                scores = dot_nt(k_ref[keys, :], query)
                if number == 0:
                    scores = jnp.where(diagonal((BLOCK, BLOCK)), scores, -1e30)
                probs.append(jnp.exp(scores - lse))
                grads.append(dot_nt(v_ref[keys, :], grad))
            centre = sum(
                jnp.sum(prob * prob_grad, axis=0, keepdims=True)
                for prob, prob_grad in zip(probs, grads)
            )
            turned = jnp.zeros((HD, BLOCK), F32)
            for keys, prob, prob_grad in zip(parts, probs, grads):
                score_grad = (prob * (prob_grad - centre)).astype(BF16)
                dv_ref[keys, :] += dot_nn(prob.astype(BF16), grad)
                dk_ref[keys, :] += dot_nn(score_grad, query)
                turned = turned + dot_nn(kt_ref[:, keys], score_grad)
            out_ref[outside, 0:HD] = unturn(rows, jnp.transpose(turned) * scale).astype(BF16)

        @pl.when(before >= length)
        def _(outside=outside):
            out_ref[outside, 0:HD] = jnp.zeros((BLOCK, HD), BF16)

    for index in range(SEQ // BLOCK):
        rows = pl.ds(index * BLOCK, BLOCK)
        outside = local_rows(index, place)
        out_ref[outside, HD : 2 * HD] = unturn(rows, dk_ref[rows, :]).astype(BF16)
        out_ref[outside, 2 * HD : 3 * HD] = dv_ref[rows, :].astype(BF16)


def attend_back(queries, key_rows, value_rows, grad, lse, length, tables):
    heads = queries.shape[1] // HD
    table_spec = pl.BlockSpec((SEQ, HD), lambda h, n: (0, 0), pipeline_mode=pl.Buffered(1))
    head_spec = pl.BlockSpec((SEQ, HD), lambda h, n: (0, h))
    pairs = heads * SEQ * SEQ // 2
    return pl.pallas_call(
        attend_back_kernel,
        out_shape=jax.ShapeDtypeStruct((SEQ, heads * 3 * HD), BF16),
        grid_spec=pltpu.PrefetchScalarGridSpec(
            num_scalar_prefetch=1,
            grid=(heads,),
            in_specs=[head_spec] * 4
            + [pl.BlockSpec((1, 1, SEQ), lambda h, n: (h, 0, 0))]
            + [table_spec] * 3,
            out_specs=pl.BlockSpec((SEQ, 3 * HD), lambda h, n: (0, h)),
            scratch_shapes=[
                pltpu.VMEM((HD, SEQ), BF16),
                pltpu.VMEM((SEQ, HD), F32),
                pltpu.VMEM((SEQ, HD), F32),
            ],
        ),
        compiler_params=pltpu.CompilerParams(vmem_limit_bytes=56 << 20),
        cost_estimate=pl.CostEstimate(
            flops=340 * HINT * pairs, transcendentals=0, bytes_accessed=heads * SEQ * HD * 14
        ),
        name="attend_back",
    )(length, queries, key_rows, value_rows, grad, lse, *tables)


def hold(*values):
    return lax.optimization_barrier(values)


def swap_tensor(values, bit):
    count = lax.axis_size("tensor")
    return lax.ppermute(values, "tensor", [(t, t ^ bit) for t in range(count)])


def block_mask():
    return lax.axis_index("tensor") if lax.axis_size("tensor") == 4 else jnp.int32(0)


def near_blocks(block):
    if lax.axis_size("tensor") != 4:
        return [lax.all_gather(block, "tensor", axis=0, tiled=True)], None
    return [block, swap_tensor(block, 1)], swap_tensor(block, 2)


def far_blocks(far):
    return [far, swap_tensor(far, 1)]


def scatter_stages(sent, kept=None):
    if kept is None:
        (sent,) = yield (sent,)
        total = lax.psum_scatter(sent, "tensor", scatter_dimension=0, tiled=True)
        for _ in range(3):
            (total,) = yield (total,)
        return total.astype(F32)
    kept, sent = yield kept, sent
    kept, got = yield kept, swap_tensor(sent, 1)
    rows = kept.shape[0] // 2
    far = (kept[rows:].astype(F32) + got[rows:].astype(F32)).astype(BF16)
    far, kept, got = yield far, kept, got
    kept, got, mate = yield kept, got, swap_tensor(far, 2)
    return kept[:rows].astype(F32) + got[:rows].astype(F32) + mate.astype(F32)


def add_rows(left, right):
    return (left.astype(F32) + right.astype(F32)).astype(left.dtype)


def move_z(values, pairs):
    return lax.ppermute(values, "z", pairs)


INWARD = ((0, 1), (3, 2))
MIDDLE = ((1, 2), (2, 1))
OUTWARD = ((1, 0), (2, 3))


def on_edge():
    z = lax.axis_index("z")
    return (z == 0) | (z == 3)


def sum_line(values):
    values = add_rows(values, move_z(values, INWARD))
    values = add_rows(values, move_z(values, MIDDLE))
    return jnp.where(on_edge(), move_z(values, OUTWARD), values)


PAIRS = ((0, 1), (1, 0))


def line_stages(kept, sent):
    if lax.axis_size("z") != 4:
        for _ in range(10):
            kept, sent = yield kept, sent
        return lax.psum(kept, ("z", "y")), lax.psum(sent, ("z", "y"))
    kept, sent = yield kept, sent
    kept, got = yield kept, lax.ppermute(sent, "y", PAIRS)
    for pairs in (INWARD, MIDDLE):
        (kept,) = yield (add_rows(kept, got),)
        kept, got = yield kept, move_z(kept, pairs)
    (kept,) = yield (add_rows(kept, got),)
    kept, got = yield kept, move_z(kept, OUTWARD)
    (kept,) = yield (jnp.where(on_edge(), got, kept),)
    kept, got = yield kept, lax.ppermute(kept, "y", PAIRS)
    return kept, got


def own_half():
    return lax.axis_index("y") if lax.axis_size("z") == 4 else jnp.int32(0)


GATES = {
    "fc2_grad": ("+b",),
    "hidden_low": (),
    "fc1_low": ("a", "+a"),
    "hidden_high": ("+c",),
    "fc1_grad": ("b", "+b"),
    "packed_low": ("a", "+a", "+d"),
    "packed_high": (),
    "attend_low": ("c", "+c"),
    "attend_high": ("b", "a", "+b", "+a"),
    "dense_grad": ("d", "c", "+e", "+d", "+c"),
    "back_low": ("b", "a", "e", "+a", "+e", "+b"),
    "qkv_low": ("d", "c", "+d", "+f"),
    "back_high": ("e", "a", "b", "+e", "+c", "+b"),
    "qkv_high": ("d", "f", "+f", "+g"),
    "to_one": ("e", "c", "+e", "+n1"),
    "to_two": ("b", "f", "e", "g", "+c", "+f", "+g", "+d"),
    "to_out": ("n1", "+n2"),
}
TAIL = (
    ("f", "g", "c", "+e", "+n1", "+f"),
    ("d", "+g"),
    ("e", "+d"),
    ("n2", "+o"),
    ("f", "+n2"),
    ("g", "n1", "+g", "+f"),
    ("d",),
    ("o", "+o"),
    ("g", "n2", "+g"),
    ("f", "+s"),
    ("s", "+s"),
    ("o", "s", "+s"),
    ("g",),
    ("s", "+s"),
    ("s", "+s"),
    ("s", "+s"),
    ("s",),
)


class Piece:
    def __init__(self, stages):
        self.stages = stages
        self.waiting = next(stages)
        self.value = None
        self.fresh = True

    def step(self):
        try:
            self.waiting = self.stages.send(self.waiting)
        except StopIteration as end:
            self.value, self.waiting = end.value, ()


def hold_all(pieces, values):
    flat = list(values)
    for piece in pieces:
        flat.extend(piece.waiting)
    if not flat:
        return values
    flat = list(hold(*flat))
    start = len(values)
    for piece in pieces:
        end = start + len(piece.waiting)
        piece.waiting = tuple(flat[start:end])
        start = end
    return flat[: len(values)]


def gate(arrived, leaving, *values):
    values = hold_all(arrived, values)
    for piece in arrived:
        piece.step()
    values = hold_all([piece for piece in arrived if piece.waiting], values)
    for piece in leaving:
        piece.step()
    return values


def finish(*pieces):
    for piece in pieces:
        while piece.value is None:
            piece.step()
    return [piece.value for piece in pieces]


def small_stages(values):
    if lax.axis_size("z") != 4 or lax.axis_size("tensor") != 4:
        for _ in range(12):
            (values,) = yield (values,)
        return lax.psum(values, ("z", "y", "tensor"))
    moves = (
        lambda values: swap_tensor(values, 1),
        lambda values: swap_tensor(values, 2),
        lambda values: lax.ppermute(values, "y", PAIRS),
        lambda values: move_z(values, INWARD),
        lambda values: move_z(values, MIDDLE),
    )
    for move in moves:
        (values,) = yield (values,)
        values, got = yield values, move(values)
        values = values + got
    (values,) = yield (values,)
    values, got = yield values, move_z(values, OUTWARD)
    return jnp.where(on_edge(), got, values)


def gelu_parts(hidden):
    below = 0.5 * (1.0 + lax.erf(hidden * (0.5**0.5)))
    density = jnp.exp(-0.5 * hidden * hidden) * ((2.0 * jnp.pi) ** (-0.5))
    return hidden * below, below + hidden * density


def shards(
    inputs,
    lengths,
    ln1_gain,
    ln1_bias,
    ln2_gain,
    ln2_bias,
    w_qkv,
    b_qkv,
    w_dense,
    b_dense,
    w_fc1,
    b_fc1,
    w_fc2,
    b_fc2,
    out_grad,
):
    width = inputs.shape[1]
    tables = rotary_tables()
    scalars = jnp.stack([lengths[0], block_mask()])
    upper = own_half()
    half = width // 2
    near_in, far_in = near_blocks(inputs)
    near_low, far_low = near_blocks(out_grad[:, :half])
    near_high, far_high = near_blocks(out_grad[:, half:])
    vectors = [v.astype(F32)[None] for v in (ln1_gain, ln1_bias, ln2_gain, ln2_bias)]
    bias = b_fc1.astype(F32)[None]
    whole = SEQ
    split = far_in is not None
    parts = 2 if split else 1
    whole_one, whole_two = normalize(near_in, vectors, whole, 0)
    hidden, active = feed_forward(whole_two, w_fc1, bias, 0, parts)
    if far_in is not None:
        far_in, whole_one, whole_two, hidden, active = hold(
            far_in, whole_one, whole_two, hidden, active
        )
        whole_one, whole_two = normalize(
            far_blocks(far_in), vectors, whole, 1, (whole_one, whole_two)
        )
        hidden, active = feed_forward(whole_two, w_fc1, bias, 1, parts, (hidden, active))
        far_low, active = hold(far_low, active)
        near_low = near_low + far_blocks(far_low)
    grad_low = stack_rows(near_low)

    def half_gradient(left, right, side):
        rows = left.shape[1] // 2
        return dot_tn(lax.dynamic_slice_in_dim(left, side * rows, rows, 1), right).astype(BF16)

    def gradient(left, right):
        return hold(half_gradient(left, right, 1 - upper), left, right)

    def keep(left, right):
        return half_gradient(left, right, upper)

    token = scalars
    pieces = {}

    weights = {"a": "fc2", "b": "fc2", "c": "fc1", "d": "fc1", "e": "dense", "f": "qkv", "g": "qkv"}
    sums = {}

    def proceed(names, *values):
        ready = list(sums)
        came = [name for name in names if name[0] != "+"]
        leave = [pieces[name[1:]] for name in names if name[0] == "+"]
        arrived = [pieces[name] for name in came]
        values = hold_all([piece for piece in pieces.values() if piece.fresh], values)
        for piece in pieces.values():
            piece.fresh = False
        results = gate(arrived, leave, *values, *[sums[name] for name in ready])
        sums.update(zip(ready, results[len(values) :]))
        for name in came:
            weight = weights.get(name)
            if weight and pieces[name].value is not None:
                column = int(name in "bdg")
                sums[weight] = assemble(
                    pieces[name].value,
                    upper,
                    column,
                    1 if weight == "dense" else 2,
                    sums.get(weight),
                )
        return results[: len(values)]

    def at(place, *values):
        return proceed(GATES[place], *values)

    sent_a, active, grad_low = gradient(active, grad_low)
    kept_a = keep(active, grad_low)
    pieces["a"] = Piece(line_stages(kept_a, sent_a))
    pieces["a"].step()
    pieces["a"].fresh = False
    if far_high is not None:
        far_high, kept_a = hold(far_high, kept_a)
        near_high = near_high + far_blocks(far_high)
    grad_high = stack_rows(near_high)
    sent_b, kept_b = gradients(active, grad_high, upper)
    pieces["b"] = Piece(line_stages(kept_b, sent_b))
    grad_low, grad_high, kept_b, sent_b = at("fc2_grad", grad_low, grad_high, kept_b, sent_b)
    wide = w_fc2.shape[0] // 2

    def hidden_back(part, low, high):
        shape = (wide, half)
        return matmul(
            "nt",
            [(low, (w_fc2, shape, (part, 0))), (high, (w_fc2, shape, (part, 1)))],
            BF16,
            256,
            extras=[(hidden, part)],
            finish=lambda total, rows: total * gelu_parts(rows)[1],
            chunk=512,
            name="hidden_grad",
        )

    hidden_low = hidden_back(0, grad_low, grad_high)
    hidden_low, whole_two, grad_low = at("hidden_low", hidden_low, whole_two, grad_low)
    sent_c, kept_c = gradients(whole_two, hidden_low, upper)
    pieces["c"] = Piece(line_stages(kept_c, sent_c))
    kept_c, sent_c, grad_low = at("fc1_low", kept_c, sent_c, grad_low)
    hidden_high = hidden_back(1, grad_low, grad_high)
    hidden_high, whole_two = at("hidden_high", hidden_high, whole_two)
    sent_d, kept_d = gradients(whole_two, hidden_high, upper)
    fc1_bias_grad = jnp.concatenate(
        [jnp.sum(part, axis=0, dtype=F32) for part in (hidden_low, hidden_high)]
    )
    pieces["d"] = Piece(line_stages(kept_d, sent_d))
    kept_d, sent_d, whole_one = at("fc1_grad", kept_d, sent_d, whole_one)

    columns = w_qkv.shape[1] // 2

    def project(part, rows):
        return matmul(
            "nn",
            [(rows, (w_qkv, (width, columns), (0, part)))],
            F32,
            512,
            extras=[b_qkv[part * columns : (part + 1) * columns].astype(F32)[None]],
            finish=jnp.add,
            name="packed",
        )

    packed_low = project(0, whole_one)
    packed_low, whole_one = at("packed_low", packed_low, whole_one)
    packed_high = project(1, whole_one)
    packed_low, packed_high = at("packed_high", packed_low, packed_high)
    saved_low = attend(packed_low, scalars, tables)
    packed_high, *saved_low = at("attend_low", packed_high, *saved_low)
    saved_high = attend(packed_high, scalars, tables)
    context = jnp.concatenate([saved_low[3], saved_high[3]], axis=1)
    context, grad_low = at("attend_high", context, grad_low)
    sent_low, kept_low = gradients(context, grad_low, upper)
    sent_high, kept_high = gradients(context, grad_high, upper)
    sent_e = jnp.concatenate([sent_low, sent_high], axis=1)
    kept_e = jnp.concatenate([kept_low, kept_high], axis=1)
    inner = w_dense.shape[0] // 2
    pieces["e"] = Piece(line_stages(kept_e, sent_e))
    grad_low, kept_e, sent_e = at("dense_grad", grad_low, kept_e, sent_e)

    def back(part, saved, low):
        shape = (inner, half)
        grad = matmul(
            "nt",
            [(low, (w_dense, shape, (part, 0))), (grad_high, (w_dense, shape, (part, 1)))],
            BF16,
            512,
            name="context_grad",
        )
        queries, key_rows, value_rows, _, lse = saved
        return attend_back(queries, key_rows, value_rows, grad, lse, scalars, tables)

    back_low = back(0, saved_low, grad_low)
    back_low, grad_low, whole_one = at("back_low", back_low, grad_low, whole_one)
    sent_f, kept_f = gradients(whole_one, back_low, upper)
    pieces["f"] = Piece(line_stages(kept_f, sent_f))
    kept_f, sent_f, grad_low = at("qkv_low", kept_f, sent_f, grad_low)
    back_high = back(1, saved_high, grad_low)
    back_high, whole_one = at("back_high", back_high, whole_one)
    sent_g, kept_g = gradients(whole_one, back_high, upper)
    packed_grad = jnp.concatenate([back_low, back_high], axis=1)
    qkv_bias_grad = jnp.sum(packed_grad, axis=0, dtype=F32)
    pieces["g"] = Piece(line_stages(kept_g, sent_g))
    packed_grad, kept_g, sent_g = at("qkv_high", packed_grad, kept_g, sent_g)
    to_one = matmul("nt", [(packed_grad, w_qkv)], BF16, 512, split=split, name="to_one")
    pieces["n1"] = Piece(scatter_stages(*to_one) if split else scatter_stages(to_one))
    (hidden_low,) = at("to_one", hidden_low)
    to_two = matmul(
        "nt",
        [
            (hidden_low, (w_fc1, (width, wide), (0, 0))),
            (hidden_high, (w_fc1, (width, wide), (0, 1))),
        ],
        BF16,
        512,
        split=split,
        name="to_two",
    )
    pieces["n2"] = Piece(scatter_stages(*to_two) if split else scatter_stages(to_two))
    context, active = at("to_two", context, active)
    to_out = matmul(
        "nn", [(context, w_dense), (active, w_fc2)], BF16, 512, split=split, name="to_out"
    )
    pieces["o"] = Piece(scatter_stages(*to_out) if split else scatter_stages(to_out))
    (token,) = at("to_out", token)

    own_rows = inputs.astype(F32)
    own_grad = out_grad.astype(F32)

    def norms_back(normed_one, normed_two):
        middle = own_rows - jnp.mean(own_rows, axis=-1, keepdims=True)
        spread = jnp.mean(middle * middle, axis=-1, keepdims=True)
        rate = lax.rsqrt(spread + EPS)
        own_hat = middle * rate

        def norm_back(grad, gain):
            scaled = grad * gain.astype(F32)
            return rate * (
                scaled
                - jnp.mean(scaled, axis=-1, keepdims=True)
                - own_hat * jnp.mean(scaled * own_hat, axis=-1, keepdims=True)
            )

        in_grad = own_grad + norm_back(normed_one, ln1_gain) + norm_back(normed_two, ln2_gain)
        shared = jnp.stack(
            [
                jnp.sum(normed_one * own_hat, axis=0),
                jnp.sum(normed_one, axis=0),
                jnp.sum(normed_two * own_hat, axis=0),
                jnp.sum(normed_two, axis=0),
                jnp.sum(own_grad, axis=0),
            ]
        )
        return in_grad, shared

    sliced = jnp.concatenate([qkv_bias_grad, fc1_bias_grad])
    place = lax.axis_index("tensor")
    slots = jnp.zeros((lax.axis_size("tensor"), sliced.shape[0]), F32)
    slots = lax.dynamic_update_slice_in_dim(slots, sliced[None], place, 0)
    common = 5 * width
    for names in TAIL:
        (token,) = proceed(names, token)
        if "s" not in pieces and None not in (pieces["n1"].value, pieces["n2"].value):
            in_grad, shared = norms_back(pieces["n1"].value, pieces["n2"].value)
            small = jnp.concatenate([shared.reshape(-1), slots.reshape(-1)]).reshape(-1, HD)
            pieces["s"] = Piece(small_stages(small))
    branches, total = finish(pieces["o"], pieces["s"])
    total = total.reshape(-1)
    vectors = total[:common].reshape(5, width)
    slots = total[common:].reshape(slots.shape)
    own_slot = lax.dynamic_index_in_dim(slots, place, 0, False)
    outputs = own_rows + branches + (b_dense.astype(F32) + b_fc2.astype(F32))
    return (
        outputs.astype(BF16),
        in_grad,
        vectors[0],
        vectors[1],
        vectors[2],
        vectors[3],
        sums["qkv"],
        own_slot[: b_qkv.shape[0]],
        sums["dense"],
        vectors[4],
        sums["fc1"],
        own_slot[b_qkv.shape[0] :],
        sums["fc2"],
        vectors[4],
    )


def solution(mesh):
    sequences, width = mesh.shape["dp"], mesh.shape["tensor"]
    mesh = Mesh(mesh.devices.reshape(sequences // 2, 2, width), ("z", "y", "tensor"))
    rows = P(("z", "y", "tensor"), None)
    columns = P(None, "tensor")
    inner = P("tensor", None)
    split = P("tensor")
    return jax.shard_map(
        shards,
        mesh=mesh,
        in_specs=(
            rows,
            P(("z", "y")),
            P(),
            P(),
            P(),
            P(),
            columns,
            split,
            inner,
            P(),
            columns,
            split,
            inner,
            P(),
            rows,
        ),
        out_specs=(
            rows,
            rows,
            P(),
            P(),
            P(),
            P(),
            columns,
            split,
            inner,
            P(),
            columns,
            split,
            inner,
            P(),
        ),
        check_vma=False,
    )
```

```python
from functools import partial

import jax
import jax.numpy as jnp
from jax import lax
from jax.experimental import pallas as pl
from jax.experimental.pallas import tpu as pltpu
from jax.sharding import Mesh
from jax.sharding import PartitionSpec as P

HD = 128
ROT = 32
SEQ = 2048
BLOCK = 512
EPS = 1e-05
HINT = 7
F32 = jnp.float32
BF16 = jnp.bfloat16


def dot_nn(left, right):
    return lax.dot_general(left, right, (((1,), (0,)), ((), ())), preferred_element_type=F32)


def dot_nt(left, right):
    return lax.dot_general(left, right, (((1,), (1,)), ((), ())), preferred_element_type=F32)


def dot_tn(left, right):
    return lax.dot_general(left, right, (((0,), (0,)), ((), ())), preferred_element_type=F32)


FORMS = {"nn": (1, 0), "nt": (1, 1)}


def matmul(form, pairs, kind, block, extras=(), finish=None, chunk=None, split=False, name=None):
    sides = FORMS[form]
    rows = pairs[0][0].shape[0]
    block = min(block, rows)
    pairs = [
        (left, right if isinstance(right, tuple) else (right, right.shape, (0, 0)))
        for left, right in pairs
    ]
    width = pairs[0][1][1][1 - sides[1]]
    dims = (((sides[0],), (sides[1],)), ((), ()))
    count = len(pairs)
    chunk = width if chunk is None else min(chunk, width)

    outs = 2 if split else 1

    def kernel(*refs):
        if split:
            for number in range(2):
                pl.when(pl.program_id(0) // 2 == number)(partial(fill, refs[:-2], refs[number - 2]))
        else:
            fill(refs[:-1], refs[-1])

    def fill(refs, out_ref):
        for start in range(0, width, chunk):
            part = slice(start, start + chunk)
            rest = [ref[:, part] for ref in refs[2 * count :]]
            total = None
            for number in range(count):
                right = refs[2 * number + 1]
                product = lax.dot_general(
                    refs[2 * number][...],
                    right[part, :] if form == "nt" else right[:, part],
                    dims,
                    preferred_element_type=F32,
                )
                total = product if total is None else total + product
            if finish is not None:
                total = finish(total, *rest)
            out_ref[:, part] = total.astype(kind)

    def at_row(i):
        return jnp.where(i < 2, 2 * i + 1, 2 * i - 4) if split else i

    specs, flat = [], []
    for left, (right, shape, index) in pairs:
        specs.append(pl.BlockSpec((block, left.shape[1]), lambda i: (at_row(i), 0)))
        specs.append(
            pl.BlockSpec(shape, lambda i, index=index: index, pipeline_mode=pl.Buffered(1))
        )
        flat.extend([left, right])
    for extra in extras:
        if isinstance(extra, tuple):
            extra, column = extra
            specs.append(pl.BlockSpec((block, width), lambda i, column=column: (i, column)))
        else:
            specs.append(pl.BlockSpec(extra.shape, lambda i: (0, 0)))
        flat.append(extra)
    inner = sum(left.shape[1] for left, _ in pairs)
    if split:
        out_specs = (
            pl.BlockSpec((block, width), lambda i: (jnp.minimum(i, 1), 0)),
            pl.BlockSpec((block, width), lambda i: (jnp.maximum(i - 2, 0), 0)),
        )
    else:
        out_specs = (pl.BlockSpec((block, width), lambda i: (i, 0)),)
    results = pl.pallas_call(
        kernel,
        out_shape=(jax.ShapeDtypeStruct((rows // outs, width), kind),) * outs,
        grid=(rows // block,),
        in_specs=specs,
        out_specs=out_specs,
        compiler_params=pltpu.CompilerParams(vmem_limit_bytes=56 << 20),
        cost_estimate=pl.CostEstimate(
            flops=rows * width * inner * HINT // 8, transcendentals=0, bytes_accessed=rows * width
        ),
        name=name,
    )(*flat)
    return results if split else results[0]


def gradient_kernel(upper_ref, left_ref, right_ref, sent_ref, kept_ref):
    product = lax.dot_general(
        left_ref[...], right_ref[...], (((0,), (0,)), ((), ())), preferred_element_type=F32
    ).astype(BF16)

    @pl.when(pl.program_id(0) == 0)
    def _():
        sent_ref[...] = product

    @pl.when(pl.program_id(0) == 1)
    def _():
        kept_ref[...] = product


def gradients(left, right, upper):
    height, width = left.shape[1] // 2, right.shape[1]
    block = min(512, height)
    steps = height // block
    shape = jax.ShapeDtypeStruct((height, width), BF16)
    return pl.pallas_call(
        gradient_kernel,
        out_shape=(shape, shape),
        grid_spec=pltpu.PrefetchScalarGridSpec(
            num_scalar_prefetch=1,
            grid=(2, steps),
            in_specs=[
                pl.BlockSpec(
                    (left.shape[0], block),
                    lambda s, i, u: (0, jnp.where(s == 0, 1 - u[0], u[0]) * steps + i),
                ),
                pl.BlockSpec(right.shape, lambda s, i, u: (0, 0), pipeline_mode=pl.Buffered(1)),
            ],
            out_specs=(
                pl.BlockSpec((block, width), lambda s, i, u: (jnp.where(s == 0, i, steps - 1), 0)),
                pl.BlockSpec((block, width), lambda s, i, u: (jnp.where(s == 0, 0, i), 0)),
            ),
        ),
        compiler_params=pltpu.CompilerParams(vmem_limit_bytes=48 << 20),
        cost_estimate=pl.CostEstimate(
            flops=2 * height * width * left.shape[0] * HINT // 8,
            transcendentals=0,
            bytes_accessed=height * width,
        ),
        name="gradients",
    )(upper[None], left, right)


def stack_kernel(*refs):
    for number in range(len(refs) - 1):

        @pl.when(pl.program_id(0) == number)
        def _(number=number):
            refs[-1][...] = refs[number][...]


def stack_rows(blocks):
    rows, width = blocks[0].shape
    return pl.pallas_call(
        stack_kernel,
        out_shape=jax.ShapeDtypeStruct((rows * len(blocks), width), blocks[0].dtype),
        grid=(len(blocks),),
        in_specs=[pl.BlockSpec((rows, width), lambda i: (0, 0))] * len(blocks),
        out_specs=pl.BlockSpec((rows, width), lambda i: (i, 0)),
        compiler_params=pltpu.CompilerParams(vmem_limit_bytes=32 << 20),
        name="stack_rows",
    )(*blocks)


def normalize_kernel(*refs, blocks):
    gains = [ref[...] for ref in refs[blocks : blocks + 4]]
    for number in range(blocks):

        @pl.when(pl.program_id(0) == number)
        def _(number=number):
            rows = refs[number][...].astype(F32)
            middle = rows - jnp.mean(rows, axis=-1, keepdims=True)
            spread = jnp.mean(middle * middle, axis=-1, keepdims=True)
            middle = middle * lax.rsqrt(spread + EPS)
            refs[-2][...] = (middle * gains[0] + gains[1]).astype(BF16)
            refs[-1][...] = (middle * gains[2] + gains[3]).astype(BF16)


def normalize(blocks, vectors, total, place, buffers=()):
    rows, width = blocks[0].shape
    step = min(256, rows)
    steps = rows // step
    count = len(blocks)

    def pick(number):
        return lambda s, i: (
            jnp.where(s == number, i, jnp.where(s < number, 0, steps - 1)),
            0,
        )

    shape = jax.ShapeDtypeStruct((total, width), BF16)
    out_spec = pl.BlockSpec((step, width), lambda s, i: ((place * count + s) * steps + i, 0))
    return pl.pallas_call(
        partial(normalize_kernel, blocks=count),
        out_shape=(shape, shape),
        grid=(count, steps),
        in_specs=[pl.BlockSpec((step, width), pick(number)) for number in range(count)]
        + [pl.BlockSpec((1, width), lambda s, i: (0, 0))] * 4
        + [pl.BlockSpec(memory_space=pl.ANY)] * len(buffers),
        out_specs=(out_spec, out_spec),
        input_output_aliases={count + 4 + n: n for n in range(len(buffers))},
        compiler_params=pltpu.CompilerParams(vmem_limit_bytes=40 << 20),
        name="normalize",
    )(*blocks, *vectors, *buffers)


def feed_forward_kernel(rows_ref, weight_ref, bias_ref, *refs, chunk):
    hidden_ref, active_ref = refs[-2:]
    for start in range(0, weight_ref.shape[1], chunk):
        part = slice(start, start + chunk)
        hidden = dot_nn(rows_ref[...], weight_ref[:, part]) + bias_ref[:, part]
        hidden_ref[:, part] = hidden
        active_ref[:, part] = gelu_parts(hidden)[0].astype(BF16)


def feed_forward(rows_in, weight, bias, place, parts, buffers=()):
    total, width = rows_in.shape
    wide = weight.shape[1]
    step = min(256, total)
    steps = total // step // parts
    out_spec = pl.BlockSpec((step, wide), lambda i: (place * steps + i, 0))
    return pl.pallas_call(
        partial(feed_forward_kernel, chunk=min(512, wide)),
        out_shape=(
            jax.ShapeDtypeStruct((total, wide), F32),
            jax.ShapeDtypeStruct((total, wide), BF16),
        ),
        grid=(steps,),
        in_specs=[
            pl.BlockSpec((step, width), lambda i: (place * steps + i, 0)),
            pl.BlockSpec(weight.shape, lambda i: (0, 0), pipeline_mode=pl.Buffered(1)),
            pl.BlockSpec((1, wide), lambda i: (0, 0)),
        ]
        + [pl.BlockSpec(memory_space=pl.ANY)] * len(buffers),
        out_specs=(out_spec, out_spec),
        input_output_aliases={3 + n: n for n in range(len(buffers))},
        compiler_params=pltpu.CompilerParams(vmem_limit_bytes=56 << 20),
        name="feed_forward",
    )(rows_in, weight, bias, *buffers)


def assemble_kernel(upper_ref, kept_ref, got_ref, *refs):
    @pl.when(pl.program_id(0) == 0)
    def _():
        refs[-1][...] = kept_ref[...].astype(F32)

    @pl.when(pl.program_id(0) == 1)
    def _():
        refs[-1][...] = got_ref[...].astype(F32)


def assemble(pair, upper, column, columns, buffer=None):
    kept, got = pair
    rows, width = kept.shape
    step = min(256, rows)
    steps = rows // step
    buffers = () if buffer is None else (buffer,)
    return pl.pallas_call(
        assemble_kernel,
        out_shape=jax.ShapeDtypeStruct((2 * rows, width * columns), F32),
        grid_spec=pltpu.PrefetchScalarGridSpec(
            num_scalar_prefetch=1,
            grid=(2, steps),
            in_specs=[
                pl.BlockSpec((step, width), lambda s, i, u: (jnp.where(s == 0, i, steps - 1), 0)),
                pl.BlockSpec((step, width), lambda s, i, u: (jnp.where(s == 0, 0, i), 0)),
            ]
            + [pl.BlockSpec(memory_space=pl.ANY)] * len(buffers),
            out_specs=pl.BlockSpec(
                (step, width),
                lambda s, i, u: (jnp.where(s == 0, u[0], 1 - u[0]) * steps + i, column),
            ),
        ),
        input_output_aliases={3: 0} if buffers else {},
        compiler_params=pltpu.CompilerParams(vmem_limit_bytes=24 << 20),
        name="assemble",
    )(upper[None], kept, got, *buffers)


def rotary_tables():
    places = jnp.arange(SEQ, dtype=F32)
    lanes = jnp.arange(HD)
    inverse = 10000.0 ** (-2.0 * (lanes % (ROT // 2)).astype(F32) / ROT)
    angles = places[:, None] * inverse[None, :]
    cosines, sines = jnp.cos(angles), jnp.sin(angles)
    turned = (lanes < ROT)[None, :]
    front = (lanes < ROT // 2)[None, :]
    cos_table = jnp.where(turned, cosines, 1.0)
    low_table = jnp.where(front, -sines, 0.0)
    high_table = jnp.where(turned & ~front, sines, 0.0)
    return cos_table, low_table, high_table


def shifted_mix(rows, low_rows, high_rows):
    half = ROT // 2
    return pltpu.roll(rows, HD - half, 1) * low_rows + pltpu.roll(rows, half, 1) * high_rows


def diagonal(shape):
    return lax.broadcasted_iota(jnp.int32, shape, 0) <= lax.broadcasted_iota(jnp.int32, shape, 1)


def local_rows(index, place):
    return pl.ds(pl.multiple_of(lax.bitwise_xor(index, place) * BLOCK, BLOCK), BLOCK)


def attend_kernel(
    length_ref, packed_ref, cos_ref, low_ref, high_ref, q_ref, k_ref, v_ref, ctx_ref, lse_ref, vt_ref
):
    length, place = length_ref[0], length_ref[1]
    scale = HD ** (-0.5)
    for index in range(SEQ // BLOCK):
        rows = pl.ds(index * BLOCK, BLOCK)
        outside = local_rows(index, place)
        cos_rows, low_rows, high_rows = cos_ref[rows, :], low_ref[rows, :], high_ref[rows, :]
        raw_query = packed_ref[outside, 0:HD]
        raw_key = packed_ref[outside, HD : 2 * HD]
        value = packed_ref[outside, 2 * HD : 3 * HD]
        query = (raw_query * cos_rows + shifted_mix(raw_query, low_rows, high_rows)) * scale
        q_ref[rows, :] = query.astype(BF16)
        key = raw_key * cos_rows + shifted_mix(raw_key, low_rows, high_rows)
        k_ref[rows, :] = key.astype(BF16)
        v_ref[rows, :] = value.astype(BF16)
        vt_ref[:, rows] = jnp.transpose(value).astype(BF16)
    for index in range(SEQ // BLOCK):
        before = index * BLOCK
        rows = pl.ds(before, BLOCK)
        outside = local_rows(index, place)

        @pl.when(before < length)
        def _(before=before, rows=rows, outside=outside):
            query = q_ref[rows, :]
            near = jnp.where(diagonal((BLOCK, BLOCK)), dot_nt(k_ref[rows, :], query), -1e30)
            highest = jnp.max(near, axis=0, keepdims=True)
            if before:
                far = dot_nt(k_ref[0:before, :], query)
                highest = jnp.maximum(highest, jnp.max(far, axis=0, keepdims=True))
            near = jnp.exp(near - highest)
            totals = jnp.sum(near, axis=0, keepdims=True)
            if before:
                far = jnp.exp(far - highest)
                totals = totals + jnp.sum(far, axis=0, keepdims=True)
            inverse = 1.0 / totals
            turned = dot_nn(vt_ref[:, rows], (near * inverse).astype(BF16))
            if before:
                turned = turned + dot_nn(vt_ref[:, 0:before], (far * inverse).astype(BF16))
            context = jnp.transpose(turned)
            places = before + lax.broadcasted_iota(jnp.int32, (BLOCK, HD), 0)
            ctx_ref[outside, :] = jnp.where(places < length, context, 0.0).astype(BF16)
            lse_ref[0, :, rows] = highest + jnp.log(totals)

        @pl.when(before >= length)
        def _(rows=rows, outside=outside):
            ctx_ref[outside, :] = jnp.zeros((BLOCK, HD), BF16)
            lse_ref[0, :, rows] = jnp.zeros((1, BLOCK), F32)


def attend(packed, length, tables):
    heads = packed.shape[1] // (3 * HD)
    table_spec = pl.BlockSpec((SEQ, HD), lambda h, n: (0, 0), pipeline_mode=pl.Buffered(1))
    head_spec = pl.BlockSpec((SEQ, HD), lambda h, n: (0, h))
    rows = jax.ShapeDtypeStruct((SEQ, heads * HD), BF16)
    pairs = heads * SEQ * SEQ // 2
    return pl.pallas_call(
        attend_kernel,
        out_shape=(rows, rows, rows, rows, jax.ShapeDtypeStruct((heads, 1, SEQ), F32)),
        grid_spec=pltpu.PrefetchScalarGridSpec(
            num_scalar_prefetch=1,
            grid=(heads,),
            in_specs=[pl.BlockSpec((SEQ, 3 * HD), lambda h, n: (0, h))] + [table_spec] * 3,
            out_specs=[head_spec] * 4 + [pl.BlockSpec((1, 1, SEQ), lambda h, n: (h, 0, 0))],
            scratch_shapes=[pltpu.VMEM((HD, SEQ), BF16)],
        ),
        compiler_params=pltpu.CompilerParams(vmem_limit_bytes=56 << 20),
        cost_estimate=pl.CostEstimate(
            flops=240 * HINT * pairs, transcendentals=0, bytes_accessed=heads * SEQ * HD * 20
        ),
        name="attend",
    )(length, packed, *tables)


def attend_back_kernel(
    length_ref,
    q_ref,
    k_ref,
    v_ref,
    grad_ref,
    lse_ref,
    cos_ref,
    low_ref,
    high_ref,
    out_ref,
    kt_ref,
    dk_ref,
    dv_ref,
):
    length, place = length_ref[0], length_ref[1]
    scale = HD ** (-0.5)
    kt_ref[...] = jnp.transpose(k_ref[...].astype(F32)).astype(BF16)
    dk_ref[...] = jnp.zeros_like(dk_ref)
    dv_ref[...] = jnp.zeros_like(dv_ref)

    def unturn(rows, grad):
        return grad * cos_ref[rows, :] - shifted_mix(grad, low_ref[rows, :], high_ref[rows, :])

    for index in range(SEQ // BLOCK):
        before = index * BLOCK
        rows = pl.ds(before, BLOCK)
        outside = local_rows(index, place)

        @pl.when(before < length)
        def _(before=before, rows=rows, outside=outside):
            query = q_ref[rows, :]
            places = before + lax.broadcasted_iota(jnp.int32, (BLOCK, HD), 0)
            grad = jnp.where(places < length, grad_ref[outside, :].astype(F32), 0.0).astype(BF16)
            lse = lse_ref[0, :, rows]
            parts = [rows] + ([pl.ds(0, before)] if before else [])
            probs, grads = [], []
            for number, keys in enumerate(parts):
                scores = dot_nt(k_ref[keys, :], query)
                if number == 0:
                    scores = jnp.where(diagonal((BLOCK, BLOCK)), scores, -1e30)
                probs.append(jnp.exp(scores - lse))
                grads.append(dot_nt(v_ref[keys, :], grad))
            centre = sum(
                jnp.sum(prob * prob_grad, axis=0, keepdims=True)
                for prob, prob_grad in zip(probs, grads)
            )
            turned = jnp.zeros((HD, BLOCK), F32)
            for keys, prob, prob_grad in zip(parts, probs, grads):
                score_grad = (prob * (prob_grad - centre)).astype(BF16)
                dv_ref[keys, :] += dot_nn(prob.astype(BF16), grad)
                dk_ref[keys, :] += dot_nn(score_grad, query)
                turned = turned + dot_nn(kt_ref[:, keys], score_grad)
            out_ref[outside, 0:HD] = unturn(rows, jnp.transpose(turned) * scale).astype(BF16)

        @pl.when(before >= length)
        def _(outside=outside):
            out_ref[outside, 0:HD] = jnp.zeros((BLOCK, HD), BF16)

    for index in range(SEQ // BLOCK):
        rows = pl.ds(index * BLOCK, BLOCK)
        outside = local_rows(index, place)
        out_ref[outside, HD : 2 * HD] = unturn(rows, dk_ref[rows, :]).astype(BF16)
        out_ref[outside, 2 * HD : 3 * HD] = dv_ref[rows, :].astype(BF16)


def attend_back(queries, key_rows, value_rows, grad, lse, length, tables):
    heads = queries.shape[1] // HD
    table_spec = pl.BlockSpec((SEQ, HD), lambda h, n: (0, 0), pipeline_mode=pl.Buffered(1))
    head_spec = pl.BlockSpec((SEQ, HD), lambda h, n: (0, h))
    pairs = heads * SEQ * SEQ // 2
    return pl.pallas_call(
        attend_back_kernel,
        out_shape=jax.ShapeDtypeStruct((SEQ, heads * 3 * HD), BF16),
        grid_spec=pltpu.PrefetchScalarGridSpec(
            num_scalar_prefetch=1,
            grid=(heads,),
            in_specs=[head_spec] * 4
            + [pl.BlockSpec((1, 1, SEQ), lambda h, n: (h, 0, 0))]
            + [table_spec] * 3,
            out_specs=pl.BlockSpec((SEQ, 3 * HD), lambda h, n: (0, h)),
            scratch_shapes=[
                pltpu.VMEM((HD, SEQ), BF16),
                pltpu.VMEM((SEQ, HD), F32),
                pltpu.VMEM((SEQ, HD), F32),
            ],
        ),
        compiler_params=pltpu.CompilerParams(vmem_limit_bytes=56 << 20),
        cost_estimate=pl.CostEstimate(
            flops=340 * HINT * pairs, transcendentals=0, bytes_accessed=heads * SEQ * HD * 14
        ),
        name="attend_back",
    )(length, queries, key_rows, value_rows, grad, lse, *tables)


def hold(*values):
    return lax.optimization_barrier(values)


def swap_tensor(values, bit):
    count = lax.axis_size("tensor")
    return lax.ppermute(values, "tensor", [(t, t ^ bit) for t in range(count)])


def block_mask():
    return lax.axis_index("tensor") if lax.axis_size("tensor") == 4 else jnp.int32(0)


def near_blocks(block):
    if lax.axis_size("tensor") != 4:
        return [lax.all_gather(block, "tensor", axis=0, tiled=True)], None
    return [block, swap_tensor(block, 1)], swap_tensor(block, 2)


def far_blocks(far):
    return [far, swap_tensor(far, 1)]


def scatter_stages(sent, kept=None):
    if kept is None:
        (sent,) = yield (sent,)
        total = lax.psum_scatter(sent, "tensor", scatter_dimension=0, tiled=True)
        for _ in range(3):
            (total,) = yield (total,)
        return total.astype(F32)
    kept, sent = yield kept, sent
    kept, got = yield kept, swap_tensor(sent, 1)
    rows = kept.shape[0] // 2
    far = (kept[rows:].astype(F32) + got[rows:].astype(F32)).astype(BF16)
    far, kept, got = yield far, kept, got
    kept, got, mate = yield kept, got, swap_tensor(far, 2)
    return kept[:rows].astype(F32) + got[:rows].astype(F32) + mate.astype(F32)


def add_rows(left, right):
    return (left.astype(F32) + right.astype(F32)).astype(left.dtype)


def move_z(values, pairs):
    return lax.ppermute(values, "z", pairs)


INWARD = ((0, 1), (3, 2))
MIDDLE = ((1, 2), (2, 1))
OUTWARD = ((1, 0), (2, 3))


def on_edge():
    z = lax.axis_index("z")
    return (z == 0) | (z == 3)


def sum_line(values):
    values = add_rows(values, move_z(values, INWARD))
    values = add_rows(values, move_z(values, MIDDLE))
    return jnp.where(on_edge(), move_z(values, OUTWARD), values)


PAIRS = ((0, 1), (1, 0))


def line_stages(kept, sent):
    if lax.axis_size("z") != 4:
        for _ in range(10):
            kept, sent = yield kept, sent
        return lax.psum(kept, ("z", "y")), lax.psum(sent, ("z", "y"))
    kept, sent = yield kept, sent
    kept, got = yield kept, lax.ppermute(sent, "y", PAIRS)
    for pairs in (INWARD, MIDDLE):
        (kept,) = yield (add_rows(kept, got),)
        kept, got = yield kept, move_z(kept, pairs)
    (kept,) = yield (add_rows(kept, got),)
    kept, got = yield kept, move_z(kept, OUTWARD)
    (kept,) = yield (jnp.where(on_edge(), got, kept),)
    kept, got = yield kept, lax.ppermute(kept, "y", PAIRS)
    return kept, got


def own_half():
    return lax.axis_index("y") if lax.axis_size("z") == 4 else jnp.int32(0)


GATES = {
    "fc2_grad": ("+b",),
    "hidden_low": ("a", "+a"),
    "fc1_low": (),
    "hidden_high": ("+c",),
    "fc1_grad": ("b", "a", "+b", "+a"),
    "packed_low": ("+d",),
    "packed_high": (),
    "attend_low": ("c", "a", "+c", "+a"),
    "attend_high": ("b", "+b"),
    "dense_grad": ("d", "c", "a", "+e", "+a", "+d", "+c"),
    "back_low": ("b", "e", "+e", "+b"),
    "qkv_low": ("d", "c", "+d", "+f"),
    "back_high": ("e", "a", "b", "+e", "+c", "+b"),
    "qkv_high": ("d", "f", "+f", "+g"),
    "to_one": ("e", "c", "b", "+e", "+n1", "+c"),
    "to_two": ("f", "e", "g", "+f", "+g", "+d"),
    "to_out": ("n1", "+n2"),
}
TAIL = (
    ("f", "g", "c", "+e", "+n1", "+f"),
    ("d", "+g"),
    ("e", "+d"),
    ("n2", "+o"),
    ("f", "+n2"),
    ("g", "n1", "+g", "+f"),
    ("d",),
    ("o", "+o"),
    ("g", "n2", "+g"),
    ("f", "+s"),
    ("s", "+s"),
    ("o", "s", "+s"),
    ("g",),
    ("s", "+s"),
    ("s", "+s"),
    ("s", "+s"),
    ("s",),
)


class Piece:
    def __init__(self, stages):
        self.stages = stages
        self.waiting = next(stages)
        self.value = None
        self.fresh = True

    def step(self):
        try:
            self.waiting = self.stages.send(self.waiting)
        except StopIteration as end:
            self.value, self.waiting = end.value, ()


def hold_all(pieces, values):
    flat = list(values)
    for piece in pieces:
        flat.extend(piece.waiting)
    if not flat:
        return values
    flat = list(hold(*flat))
    start = len(values)
    for piece in pieces:
        end = start + len(piece.waiting)
        piece.waiting = tuple(flat[start:end])
        start = end
    return flat[: len(values)]


def gate(arrived, leaving, *values):
    values = hold_all(arrived, values)
    for piece in arrived:
        piece.step()
    values = hold_all([piece for piece in arrived if piece.waiting], values)
    for piece in leaving:
        piece.step()
    return values


def finish(*pieces):
    for piece in pieces:
        while piece.value is None:
            piece.step()
    return [piece.value for piece in pieces]


def small_stages(values):
    if lax.axis_size("z") != 4 or lax.axis_size("tensor") != 4:
        for _ in range(12):
            (values,) = yield (values,)
        return lax.psum(values, ("z", "y", "tensor"))
    moves = (
        lambda values: swap_tensor(values, 1),
        lambda values: swap_tensor(values, 2),
        lambda values: lax.ppermute(values, "y", PAIRS),
        lambda values: move_z(values, INWARD),
        lambda values: move_z(values, MIDDLE),
    )
    for move in moves:
        (values,) = yield (values,)
        values, got = yield values, move(values)
        values = values + got
    (values,) = yield (values,)
    values, got = yield values, move_z(values, OUTWARD)
    return jnp.where(on_edge(), got, values)


def gelu_parts(hidden):
    below = 0.5 * (1.0 + lax.erf(hidden * (0.5**0.5)))
    density = jnp.exp(-0.5 * hidden * hidden) * ((2.0 * jnp.pi) ** (-0.5))
    return hidden * below, below + hidden * density


def shards(
    inputs,
    lengths,
    ln1_gain,
    ln1_bias,
    ln2_gain,
    ln2_bias,
    w_qkv,
    b_qkv,
    w_dense,
    b_dense,
    w_fc1,
    b_fc1,
    w_fc2,
    b_fc2,
    out_grad,
):
    width = inputs.shape[1]
    tables = rotary_tables()
    scalars = jnp.stack([lengths[0], block_mask()])
    upper = own_half()
    half = width // 2
    near_in, far_in = near_blocks(inputs)
    near_low, far_low = near_blocks(out_grad[:, :half])
    near_high, far_high = near_blocks(out_grad[:, half:])
    vectors = [v.astype(F32)[None] for v in (ln1_gain, ln1_bias, ln2_gain, ln2_bias)]
    bias = b_fc1.astype(F32)[None]
    whole = SEQ
    split = far_in is not None
    parts = 2 if split else 1
    whole_one, whole_two = normalize(near_in, vectors, whole, 0)
    hidden, active = feed_forward(whole_two, w_fc1, bias, 0, parts)
    if far_in is not None:
        far_in, whole_one, whole_two, hidden, active = hold(
            far_in, whole_one, whole_two, hidden, active
        )
        whole_one, whole_two = normalize(
            far_blocks(far_in), vectors, whole, 1, (whole_one, whole_two)
        )
        hidden, active = feed_forward(whole_two, w_fc1, bias, 1, parts, (hidden, active))
        far_low, active = hold(far_low, active)
        near_low = near_low + far_blocks(far_low)
    grad_low = stack_rows(near_low)

    def half_gradient(left, right, side):
        rows = left.shape[1] // 2
        return dot_tn(lax.dynamic_slice_in_dim(left, side * rows, rows, 1), right).astype(BF16)

    def gradient(left, right):
        return hold(half_gradient(left, right, 1 - upper), left, right)

    def keep(left, right):
        return half_gradient(left, right, upper)

    token = scalars
    pieces = {}

    weights = {"a": "fc2", "b": "fc2", "c": "fc1", "d": "fc1", "e": "dense", "f": "qkv", "g": "qkv"}
    sums = {}

    def proceed(names, *values):
        ready = list(sums)
        came = [name for name in names if name[0] != "+"]
        leave = [pieces[name[1:]] for name in names if name[0] == "+"]
        arrived = [pieces[name] for name in came]
        values = hold_all([piece for piece in pieces.values() if piece.fresh], values)
        for piece in pieces.values():
            piece.fresh = False
        results = gate(arrived, leave, *values, *[sums[name] for name in ready])
        sums.update(zip(ready, results[len(values) :]))
        for name in came:
            weight = weights.get(name)
            if weight and pieces[name].value is not None:
                column = int(name in "bdg")
                sums[weight] = assemble(
                    pieces[name].value,
                    upper,
                    column,
                    1 if weight == "dense" else 2,
                    sums.get(weight),
                )
        return results[: len(values)]

    def at(place, *values):
        return proceed(GATES[place], *values)

    sent_a, active, grad_low = gradient(active, grad_low)
    kept_a = keep(active, grad_low)
    pieces["a"] = Piece(line_stages(kept_a, sent_a))
    pieces["a"].step()
    pieces["a"].fresh = False
    if far_high is not None:
        far_high, kept_a = hold(far_high, kept_a)
        near_high = near_high + far_blocks(far_high)
    grad_high = stack_rows(near_high)
    sent_b, kept_b = gradients(active, grad_high, upper)
    pieces["b"] = Piece(line_stages(kept_b, sent_b))
    grad_low, grad_high, kept_b, sent_b = at("fc2_grad", grad_low, grad_high, kept_b, sent_b)
    wide = w_fc2.shape[0] // 2

    def hidden_back(part, low, high):
        shape = (wide, half)
        return matmul(
            "nt",
            [(low, (w_fc2, shape, (part, 0))), (high, (w_fc2, shape, (part, 1)))],
            BF16,
            256,
            extras=[(hidden, part)],
            finish=lambda total, rows: total * gelu_parts(rows)[1],
            chunk=512,
            name="hidden_grad",
        )

    hidden_low = hidden_back(0, grad_low, grad_high)
    hidden_low, whole_two, grad_low = at("hidden_low", hidden_low, whole_two, grad_low)
    sent_c, kept_c = gradients(whole_two, hidden_low, upper)
    pieces["c"] = Piece(line_stages(kept_c, sent_c))
    kept_c, sent_c, grad_low = at("fc1_low", kept_c, sent_c, grad_low)
    hidden_high = hidden_back(1, grad_low, grad_high)
    hidden_high, whole_two = at("hidden_high", hidden_high, whole_two)
    sent_d, kept_d = gradients(whole_two, hidden_high, upper)
    fc1_bias_grad = jnp.concatenate(
        [jnp.sum(part, axis=0, dtype=F32) for part in (hidden_low, hidden_high)]
    )
    pieces["d"] = Piece(line_stages(kept_d, sent_d))
    kept_d, sent_d, whole_one = at("fc1_grad", kept_d, sent_d, whole_one)

    columns = w_qkv.shape[1] // 2

    def project(part, rows):
        return matmul(
            "nn",
            [(rows, (w_qkv, (width, columns), (0, part)))],
            F32,
            512,
            extras=[b_qkv[part * columns : (part + 1) * columns].astype(F32)[None]],
            finish=jnp.add,
            name="packed",
        )

    packed_low = project(0, whole_one)
    packed_low, whole_one = at("packed_low", packed_low, whole_one)
    packed_high = project(1, whole_one)
    packed_low, packed_high = at("packed_high", packed_low, packed_high)
    saved_low = attend(packed_low, scalars, tables)
    packed_high, *saved_low = at("attend_low", packed_high, *saved_low)
    saved_high = attend(packed_high, scalars, tables)
    context = jnp.concatenate([saved_low[3], saved_high[3]], axis=1)
    context, grad_low = at("attend_high", context, grad_low)
    sent_low, kept_low = gradients(context, grad_low, upper)
    sent_high, kept_high = gradients(context, grad_high, upper)
    sent_e = jnp.concatenate([sent_low, sent_high], axis=1)
    kept_e = jnp.concatenate([kept_low, kept_high], axis=1)
    inner = w_dense.shape[0] // 2
    pieces["e"] = Piece(line_stages(kept_e, sent_e))
    grad_low, kept_e, sent_e = at("dense_grad", grad_low, kept_e, sent_e)

    def back(part, saved, low):
        shape = (inner, half)
        grad = matmul(
            "nt",
            [(low, (w_dense, shape, (part, 0))), (grad_high, (w_dense, shape, (part, 1)))],
            BF16,
            512,
            name="context_grad",
        )
        queries, key_rows, value_rows, _, lse = saved
        return attend_back(queries, key_rows, value_rows, grad, lse, scalars, tables)

    back_low = back(0, saved_low, grad_low)
    back_low, grad_low, whole_one = at("back_low", back_low, grad_low, whole_one)
    sent_f, kept_f = gradients(whole_one, back_low, upper)
    pieces["f"] = Piece(line_stages(kept_f, sent_f))
    kept_f, sent_f, grad_low = at("qkv_low", kept_f, sent_f, grad_low)
    back_high = back(1, saved_high, grad_low)
    back_high, whole_one = at("back_high", back_high, whole_one)
    sent_g, kept_g = gradients(whole_one, back_high, upper)
    packed_grad = jnp.concatenate([back_low, back_high], axis=1)
    qkv_bias_grad = jnp.sum(packed_grad, axis=0, dtype=F32)
    pieces["g"] = Piece(line_stages(kept_g, sent_g))
    packed_grad, kept_g, sent_g = at("qkv_high", packed_grad, kept_g, sent_g)
    to_one = matmul("nt", [(packed_grad, w_qkv)], BF16, 512, split=split, name="to_one")
    pieces["n1"] = Piece(scatter_stages(*to_one) if split else scatter_stages(to_one))
    (hidden_low,) = at("to_one", hidden_low)
    to_two = matmul(
        "nt",
        [
            (hidden_low, (w_fc1, (width, wide), (0, 0))),
            (hidden_high, (w_fc1, (width, wide), (0, 1))),
        ],
        BF16,
        512,
        split=split,
        name="to_two",
    )
    pieces["n2"] = Piece(scatter_stages(*to_two) if split else scatter_stages(to_two))
    context, active = at("to_two", context, active)
    to_out = matmul(
        "nn", [(context, w_dense), (active, w_fc2)], BF16, 512, split=split, name="to_out"
    )
    pieces["o"] = Piece(scatter_stages(*to_out) if split else scatter_stages(to_out))
    (token,) = at("to_out", token)

    own_rows = inputs.astype(F32)
    own_grad = out_grad.astype(F32)

    def norms_back(normed_one, normed_two):
        middle = own_rows - jnp.mean(own_rows, axis=-1, keepdims=True)
        spread = jnp.mean(middle * middle, axis=-1, keepdims=True)
        rate = lax.rsqrt(spread + EPS)
        own_hat = middle * rate

        def norm_back(grad, gain):
            scaled = grad * gain.astype(F32)
            return rate * (
                scaled
                - jnp.mean(scaled, axis=-1, keepdims=True)
                - own_hat * jnp.mean(scaled * own_hat, axis=-1, keepdims=True)
            )

        in_grad = own_grad + norm_back(normed_one, ln1_gain) + norm_back(normed_two, ln2_gain)
        shared = jnp.stack(
            [
                jnp.sum(normed_one * own_hat, axis=0),
                jnp.sum(normed_one, axis=0),
                jnp.sum(normed_two * own_hat, axis=0),
                jnp.sum(normed_two, axis=0),
                jnp.sum(own_grad, axis=0),
            ]
        )
        return in_grad, shared

    sliced = jnp.concatenate([qkv_bias_grad, fc1_bias_grad])
    place = lax.axis_index("tensor")
    slots = jnp.zeros((lax.axis_size("tensor"), sliced.shape[0]), F32)
    slots = lax.dynamic_update_slice_in_dim(slots, sliced[None], place, 0)
    common = 5 * width
    for names in TAIL:
        (token,) = proceed(names, token)
        if "s" not in pieces and None not in (pieces["n1"].value, pieces["n2"].value):
            in_grad, shared = norms_back(pieces["n1"].value, pieces["n2"].value)
            small = jnp.concatenate([shared.reshape(-1), slots.reshape(-1)]).reshape(-1, HD)
            pieces["s"] = Piece(small_stages(small))
    branches, total = finish(pieces["o"], pieces["s"])
    total = total.reshape(-1)
    vectors = total[:common].reshape(5, width)
    slots = total[common:].reshape(slots.shape)
    own_slot = lax.dynamic_index_in_dim(slots, place, 0, False)
    outputs = own_rows + branches + (b_dense.astype(F32) + b_fc2.astype(F32))
    return (
        outputs.astype(BF16),
        in_grad,
        vectors[0],
        vectors[1],
        vectors[2],
        vectors[3],
        sums["qkv"],
        own_slot[: b_qkv.shape[0]],
        sums["dense"],
        vectors[4],
        sums["fc1"],
        own_slot[b_qkv.shape[0] :],
        sums["fc2"],
        vectors[4],
    )


def solution(mesh):
    sequences, width = mesh.shape["dp"], mesh.shape["tensor"]
    mesh = Mesh(mesh.devices.reshape(sequences // 2, 2, width), ("z", "y", "tensor"))
    rows = P(("z", "y", "tensor"), None)
    columns = P(None, "tensor")
    inner = P("tensor", None)
    split = P("tensor")
    return jax.shard_map(
        shards,
        mesh=mesh,
        in_specs=(
            rows,
            P(("z", "y")),
            P(),
            P(),
            P(),
            P(),
            columns,
            split,
            inner,
            P(),
            columns,
            split,
            inner,
            P(),
            rows,
        ),
        out_specs=(
            rows,
            rows,
            P(),
            P(),
            P(),
            P(),
            columns,
            split,
            inner,
            P(),
            columns,
            split,
            inner,
            P(),
        ),
        check_vma=False,
    )
```

```python
from functools import partial

import jax
import jax.numpy as jnp
from jax import lax
from jax.experimental import pallas as pl
from jax.experimental.pallas import tpu as pltpu
from jax.sharding import Mesh
from jax.sharding import PartitionSpec as P

HD = 128
ROT = 32
SEQ = 2048
BLOCK = 512
EPS = 1e-05
HINT = 7
F32 = jnp.float32
BF16 = jnp.bfloat16


def dot_nn(left, right):
    return lax.dot_general(left, right, (((1,), (0,)), ((), ())), preferred_element_type=F32)


def dot_nt(left, right):
    return lax.dot_general(left, right, (((1,), (1,)), ((), ())), preferred_element_type=F32)


def dot_tn(left, right):
    return lax.dot_general(left, right, (((0,), (0,)), ((), ())), preferred_element_type=F32)


FORMS = {"nn": (1, 0), "nt": (1, 1)}


def matmul(form, pairs, kind, block, extras=(), finish=None, chunk=None, split=False, name=None):
    sides = FORMS[form]
    rows = pairs[0][0].shape[0]
    block = min(block, rows)
    pairs = [
        (left, right if isinstance(right, tuple) else (right, right.shape, (0, 0)))
        for left, right in pairs
    ]
    width = pairs[0][1][1][1 - sides[1]]
    dims = (((sides[0],), (sides[1],)), ((), ()))
    count = len(pairs)
    chunk = width if chunk is None else min(chunk, width)

    outs = 2 if split else 1

    def kernel(*refs):
        if split:
            for number in range(2):
                pl.when(pl.program_id(0) // 2 == number)(partial(fill, refs[:-2], refs[number - 2]))
        else:
            fill(refs[:-1], refs[-1])

    def fill(refs, out_ref):
        for start in range(0, width, chunk):
            part = slice(start, start + chunk)
            rest = [ref[:, part] for ref in refs[2 * count :]]
            total = None
            for number in range(count):
                right = refs[2 * number + 1]
                product = lax.dot_general(
                    refs[2 * number][...],
                    right[part, :] if form == "nt" else right[:, part],
                    dims,
                    preferred_element_type=F32,
                )
                total = product if total is None else total + product
            if finish is not None:
                total = finish(total, *rest)
            out_ref[:, part] = total.astype(kind)

    def at_row(i):
        return jnp.where(i < 2, 2 * i + 1, 2 * i - 4) if split else i

    specs, flat = [], []
    for left, (right, shape, index) in pairs:
        specs.append(pl.BlockSpec((block, left.shape[1]), lambda i: (at_row(i), 0)))
        specs.append(
            pl.BlockSpec(shape, lambda i, index=index: index, pipeline_mode=pl.Buffered(1))
        )
        flat.extend([left, right])
    for extra in extras:
        if isinstance(extra, tuple):
            extra, column = extra
            specs.append(pl.BlockSpec((block, width), lambda i, column=column: (i, column)))
        else:
            specs.append(pl.BlockSpec(extra.shape, lambda i: (0, 0)))
        flat.append(extra)
    inner = sum(left.shape[1] for left, _ in pairs)
    if split:
        out_specs = (
            pl.BlockSpec((block, width), lambda i: (jnp.minimum(i, 1), 0)),
            pl.BlockSpec((block, width), lambda i: (jnp.maximum(i - 2, 0), 0)),
        )
    else:
        out_specs = (pl.BlockSpec((block, width), lambda i: (i, 0)),)
    results = pl.pallas_call(
        kernel,
        out_shape=(jax.ShapeDtypeStruct((rows // outs, width), kind),) * outs,
        grid=(rows // block,),
        in_specs=specs,
        out_specs=out_specs,
        compiler_params=pltpu.CompilerParams(vmem_limit_bytes=56 << 20),
        cost_estimate=pl.CostEstimate(
            flops=rows * width * inner * HINT // 8, transcendentals=0, bytes_accessed=rows * width
        ),
        name=name,
    )(*flat)
    return results if split else results[0]


def gradient_kernel(upper_ref, left_ref, right_ref, sent_ref, kept_ref):
    product = lax.dot_general(
        left_ref[...], right_ref[...], (((0,), (0,)), ((), ())), preferred_element_type=F32
    ).astype(BF16)

    @pl.when(pl.program_id(0) == 0)
    def _():
        sent_ref[...] = product

    @pl.when(pl.program_id(0) == 1)
    def _():
        kept_ref[...] = product


def gradients(left, right, upper):
    height, width = left.shape[1] // 2, right.shape[1]
    block = min(512, height)
    steps = height // block
    shape = jax.ShapeDtypeStruct((height, width), BF16)
    return pl.pallas_call(
        gradient_kernel,
        out_shape=(shape, shape),
        grid_spec=pltpu.PrefetchScalarGridSpec(
            num_scalar_prefetch=1,
            grid=(2, steps),
            in_specs=[
                pl.BlockSpec(
                    (left.shape[0], block),
                    lambda s, i, u: (0, jnp.where(s == 0, 1 - u[0], u[0]) * steps + i),
                ),
                pl.BlockSpec(right.shape, lambda s, i, u: (0, 0), pipeline_mode=pl.Buffered(1)),
            ],
            out_specs=(
                pl.BlockSpec((block, width), lambda s, i, u: (jnp.where(s == 0, i, steps - 1), 0)),
                pl.BlockSpec((block, width), lambda s, i, u: (jnp.where(s == 0, 0, i), 0)),
            ),
        ),
        compiler_params=pltpu.CompilerParams(vmem_limit_bytes=48 << 20),
        cost_estimate=pl.CostEstimate(
            flops=2 * height * width * left.shape[0] * HINT // 8,
            transcendentals=0,
            bytes_accessed=height * width,
        ),
        name="gradients",
    )(upper[None], left, right)


def stack_kernel(*refs):
    for number in range(len(refs) - 1):

        @pl.when(pl.program_id(0) == number)
        def _(number=number):
            refs[-1][...] = refs[number][...]


def stack_rows(blocks):
    rows, width = blocks[0].shape
    return pl.pallas_call(
        stack_kernel,
        out_shape=jax.ShapeDtypeStruct((rows * len(blocks), width), blocks[0].dtype),
        grid=(len(blocks),),
        in_specs=[pl.BlockSpec((rows, width), lambda i: (0, 0))] * len(blocks),
        out_specs=pl.BlockSpec((rows, width), lambda i: (i, 0)),
        compiler_params=pltpu.CompilerParams(vmem_limit_bytes=32 << 20),
        name="stack_rows",
    )(*blocks)


def normalize_kernel(*refs, blocks):
    gains = [ref[...] for ref in refs[blocks : blocks + 4]]
    for number in range(blocks):

        @pl.when(pl.program_id(0) == number)
        def _(number=number):
            rows = refs[number][...].astype(F32)
            middle = rows - jnp.mean(rows, axis=-1, keepdims=True)
            spread = jnp.mean(middle * middle, axis=-1, keepdims=True)
            middle = middle * lax.rsqrt(spread + EPS)
            refs[-2][...] = (middle * gains[0] + gains[1]).astype(BF16)
            refs[-1][...] = (middle * gains[2] + gains[3]).astype(BF16)


def normalize(blocks, vectors, total, place, buffers=()):
    rows, width = blocks[0].shape
    step = min(256, rows)
    steps = rows // step
    count = len(blocks)

    def pick(number):
        return lambda s, i: (
            jnp.where(s == number, i, jnp.where(s < number, 0, steps - 1)),
            0,
        )

    shape = jax.ShapeDtypeStruct((total, width), BF16)
    out_spec = pl.BlockSpec((step, width), lambda s, i: ((place * count + s) * steps + i, 0))
    return pl.pallas_call(
        partial(normalize_kernel, blocks=count),
        out_shape=(shape, shape),
        grid=(count, steps),
        in_specs=[pl.BlockSpec((step, width), pick(number)) for number in range(count)]
        + [pl.BlockSpec((1, width), lambda s, i: (0, 0))] * 4
        + [pl.BlockSpec(memory_space=pl.ANY)] * len(buffers),
        out_specs=(out_spec, out_spec),
        input_output_aliases={count + 4 + n: n for n in range(len(buffers))},
        compiler_params=pltpu.CompilerParams(vmem_limit_bytes=40 << 20),
        name="normalize",
    )(*blocks, *vectors, *buffers)


def feed_forward_kernel(rows_ref, weight_ref, bias_ref, *refs, chunk):
    hidden_ref, active_ref = refs[-2:]
    for start in range(0, weight_ref.shape[1], chunk):
        part = slice(start, start + chunk)
        hidden = dot_nn(rows_ref[...], weight_ref[:, part]) + bias_ref[:, part]
        hidden_ref[:, part] = hidden
        active_ref[:, part] = gelu_parts(hidden)[0].astype(BF16)


def feed_forward(rows_in, weight, bias, place, parts, buffers=()):
    total, width = rows_in.shape
    wide = weight.shape[1]
    step = min(256, total)
    steps = total // step // parts
    out_spec = pl.BlockSpec((step, wide), lambda i: (place * steps + i, 0))
    return pl.pallas_call(
        partial(feed_forward_kernel, chunk=min(512, wide)),
        out_shape=(
            jax.ShapeDtypeStruct((total, wide), F32),
            jax.ShapeDtypeStruct((total, wide), BF16),
        ),
        grid=(steps,),
        in_specs=[
            pl.BlockSpec((step, width), lambda i: (place * steps + i, 0)),
            pl.BlockSpec(weight.shape, lambda i: (0, 0), pipeline_mode=pl.Buffered(1)),
            pl.BlockSpec((1, wide), lambda i: (0, 0)),
        ]
        + [pl.BlockSpec(memory_space=pl.ANY)] * len(buffers),
        out_specs=(out_spec, out_spec),
        input_output_aliases={3 + n: n for n in range(len(buffers))},
        compiler_params=pltpu.CompilerParams(vmem_limit_bytes=56 << 20),
        name="feed_forward",
    )(rows_in, weight, bias, *buffers)


def assemble_kernel(upper_ref, kept_ref, got_ref, *refs):
    @pl.when(pl.program_id(0) == 0)
    def _():
        refs[-1][...] = kept_ref[...].astype(F32)

    @pl.when(pl.program_id(0) == 1)
    def _():
        refs[-1][...] = got_ref[...].astype(F32)


def assemble(pair, upper, column, columns, buffer=None):
    kept, got = pair
    rows, width = kept.shape
    step = min(256, rows)
    steps = rows // step
    buffers = () if buffer is None else (buffer,)
    return pl.pallas_call(
        assemble_kernel,
        out_shape=jax.ShapeDtypeStruct((2 * rows, width * columns), F32),
        grid_spec=pltpu.PrefetchScalarGridSpec(
            num_scalar_prefetch=1,
            grid=(2, steps),
            in_specs=[
                pl.BlockSpec((step, width), lambda s, i, u: (jnp.where(s == 0, i, steps - 1), 0)),
                pl.BlockSpec((step, width), lambda s, i, u: (jnp.where(s == 0, 0, i), 0)),
            ]
            + [pl.BlockSpec(memory_space=pl.ANY)] * len(buffers),
            out_specs=pl.BlockSpec(
                (step, width),
                lambda s, i, u: (jnp.where(s == 0, u[0], 1 - u[0]) * steps + i, column),
            ),
        ),
        input_output_aliases={3: 0} if buffers else {},
        compiler_params=pltpu.CompilerParams(vmem_limit_bytes=24 << 20),
        name="assemble",
    )(upper[None], kept, got, *buffers)


def rotary_tables():
    places = jnp.arange(SEQ, dtype=F32)
    lanes = jnp.arange(HD)
    inverse = 10000.0 ** (-2.0 * (lanes % (ROT // 2)).astype(F32) / ROT)
    angles = places[:, None] * inverse[None, :]
    cosines, sines = jnp.cos(angles), jnp.sin(angles)
    turned = (lanes < ROT)[None, :]
    front = (lanes < ROT // 2)[None, :]
    cos_table = jnp.where(turned, cosines, 1.0)
    low_table = jnp.where(front, -sines, 0.0)
    high_table = jnp.where(turned & ~front, sines, 0.0)
    return cos_table, low_table, high_table


def shifted_mix(rows, low_rows, high_rows):
    half = ROT // 2
    return pltpu.roll(rows, HD - half, 1) * low_rows + pltpu.roll(rows, half, 1) * high_rows


def diagonal(shape):
    return lax.broadcasted_iota(jnp.int32, shape, 0) <= lax.broadcasted_iota(jnp.int32, shape, 1)


def local_rows(index, place):
    return pl.ds(pl.multiple_of(lax.bitwise_xor(index, place) * BLOCK, BLOCK), BLOCK)


def attend_kernel(
    length_ref, packed_ref, cos_ref, low_ref, high_ref, q_ref, k_ref, v_ref, ctx_ref, lse_ref, vt_ref
):
    length, place = length_ref[0], length_ref[1]
    scale = HD ** (-0.5)
    for index in range(SEQ // BLOCK):
        rows = pl.ds(index * BLOCK, BLOCK)
        outside = local_rows(index, place)
        cos_rows, low_rows, high_rows = cos_ref[rows, :], low_ref[rows, :], high_ref[rows, :]
        raw_query = packed_ref[outside, 0:HD]
        raw_key = packed_ref[outside, HD : 2 * HD]
        value = packed_ref[outside, 2 * HD : 3 * HD]
        query = (raw_query * cos_rows + shifted_mix(raw_query, low_rows, high_rows)) * scale
        q_ref[rows, :] = query.astype(BF16)
        key = raw_key * cos_rows + shifted_mix(raw_key, low_rows, high_rows)
        k_ref[rows, :] = key.astype(BF16)
        v_ref[rows, :] = value.astype(BF16)
        vt_ref[:, rows] = jnp.transpose(value).astype(BF16)
    for index in range(SEQ // BLOCK):
        before = index * BLOCK
        rows = pl.ds(before, BLOCK)
        outside = local_rows(index, place)

        @pl.when(before < length)
        def _(before=before, rows=rows, outside=outside):
            query = q_ref[rows, :]
            near = jnp.where(diagonal((BLOCK, BLOCK)), dot_nt(k_ref[rows, :], query), -1e30)
            highest = jnp.max(near, axis=0, keepdims=True)
            if before:
                far = dot_nt(k_ref[0:before, :], query)
                highest = jnp.maximum(highest, jnp.max(far, axis=0, keepdims=True))
            near = jnp.exp(near - highest)
            totals = jnp.sum(near, axis=0, keepdims=True)
            if before:
                far = jnp.exp(far - highest)
                totals = totals + jnp.sum(far, axis=0, keepdims=True)
            inverse = 1.0 / totals
            turned = dot_nn(vt_ref[:, rows], (near * inverse).astype(BF16))
            if before:
                turned = turned + dot_nn(vt_ref[:, 0:before], (far * inverse).astype(BF16))
            context = jnp.transpose(turned)
            places = before + lax.broadcasted_iota(jnp.int32, (BLOCK, HD), 0)
            ctx_ref[outside, :] = jnp.where(places < length, context, 0.0).astype(BF16)
            lse_ref[0, :, rows] = highest + jnp.log(totals)

        @pl.when(before >= length)
        def _(rows=rows, outside=outside):
            ctx_ref[outside, :] = jnp.zeros((BLOCK, HD), BF16)
            lse_ref[0, :, rows] = jnp.zeros((1, BLOCK), F32)


def attend(packed, length, tables):
    heads = packed.shape[1] // (3 * HD)
    table_spec = pl.BlockSpec((SEQ, HD), lambda h, n: (0, 0), pipeline_mode=pl.Buffered(1))
    head_spec = pl.BlockSpec((SEQ, HD), lambda h, n: (0, h))
    rows = jax.ShapeDtypeStruct((SEQ, heads * HD), BF16)
    pairs = heads * SEQ * SEQ // 2
    return pl.pallas_call(
        attend_kernel,
        out_shape=(rows, rows, rows, rows, jax.ShapeDtypeStruct((heads, 1, SEQ), F32)),
        grid_spec=pltpu.PrefetchScalarGridSpec(
            num_scalar_prefetch=1,
            grid=(heads,),
            in_specs=[pl.BlockSpec((SEQ, 3 * HD), lambda h, n: (0, h))] + [table_spec] * 3,
            out_specs=[head_spec] * 4 + [pl.BlockSpec((1, 1, SEQ), lambda h, n: (h, 0, 0))],
            scratch_shapes=[pltpu.VMEM((HD, SEQ), BF16)],
        ),
        compiler_params=pltpu.CompilerParams(vmem_limit_bytes=56 << 20),
        cost_estimate=pl.CostEstimate(
            flops=240 * HINT * pairs, transcendentals=0, bytes_accessed=heads * SEQ * HD * 20
        ),
        name="attend",
    )(length, packed, *tables)


def attend_back_kernel(
    length_ref,
    q_ref,
    k_ref,
    v_ref,
    grad_ref,
    lse_ref,
    cos_ref,
    low_ref,
    high_ref,
    out_ref,
    kt_ref,
    dk_ref,
    dv_ref,
):
    length, place = length_ref[0], length_ref[1]
    scale = HD ** (-0.5)
    kt_ref[...] = jnp.transpose(k_ref[...].astype(F32)).astype(BF16)
    dk_ref[...] = jnp.zeros_like(dk_ref)
    dv_ref[...] = jnp.zeros_like(dv_ref)

    def unturn(rows, grad):
        return grad * cos_ref[rows, :] - shifted_mix(grad, low_ref[rows, :], high_ref[rows, :])

    for index in range(SEQ // BLOCK):
        before = index * BLOCK
        rows = pl.ds(before, BLOCK)
        outside = local_rows(index, place)

        @pl.when(before < length)
        def _(before=before, rows=rows, outside=outside):
            query = q_ref[rows, :]
            places = before + lax.broadcasted_iota(jnp.int32, (BLOCK, HD), 0)
            grad = jnp.where(places < length, grad_ref[outside, :].astype(F32), 0.0).astype(BF16)
            lse = lse_ref[0, :, rows]
            parts = [rows] + ([pl.ds(0, before)] if before else [])
            probs, grads = [], []
            for number, keys in enumerate(parts):
                scores = dot_nt(k_ref[keys, :], query)
                if number == 0:
                    scores = jnp.where(diagonal((BLOCK, BLOCK)), scores, -1e30)
                probs.append(jnp.exp(scores - lse))
                grads.append(dot_nt(v_ref[keys, :], grad))
            centre = sum(
                jnp.sum(prob * prob_grad, axis=0, keepdims=True)
                for prob, prob_grad in zip(probs, grads)
            )
            turned = jnp.zeros((HD, BLOCK), F32)
            for keys, prob, prob_grad in zip(parts, probs, grads):
                score_grad = (prob * (prob_grad - centre)).astype(BF16)
                dv_ref[keys, :] += dot_nn(prob.astype(BF16), grad)
                dk_ref[keys, :] += dot_nn(score_grad, query)
                turned = turned + dot_nn(kt_ref[:, keys], score_grad)
            out_ref[outside, 0:HD] = unturn(rows, jnp.transpose(turned) * scale).astype(BF16)

        @pl.when(before >= length)
        def _(outside=outside):
            out_ref[outside, 0:HD] = jnp.zeros((BLOCK, HD), BF16)

    for index in range(SEQ // BLOCK):
        rows = pl.ds(index * BLOCK, BLOCK)
        outside = local_rows(index, place)
        out_ref[outside, HD : 2 * HD] = unturn(rows, dk_ref[rows, :]).astype(BF16)
        out_ref[outside, 2 * HD : 3 * HD] = dv_ref[rows, :].astype(BF16)


def attend_back(queries, key_rows, value_rows, grad, lse, length, tables):
    heads = queries.shape[1] // HD
    table_spec = pl.BlockSpec((SEQ, HD), lambda h, n: (0, 0), pipeline_mode=pl.Buffered(1))
    head_spec = pl.BlockSpec((SEQ, HD), lambda h, n: (0, h))
    pairs = heads * SEQ * SEQ // 2
    return pl.pallas_call(
        attend_back_kernel,
        out_shape=jax.ShapeDtypeStruct((SEQ, heads * 3 * HD), BF16),
        grid_spec=pltpu.PrefetchScalarGridSpec(
            num_scalar_prefetch=1,
            grid=(heads,),
            in_specs=[head_spec] * 4
            + [pl.BlockSpec((1, 1, SEQ), lambda h, n: (h, 0, 0))]
            + [table_spec] * 3,
            out_specs=pl.BlockSpec((SEQ, 3 * HD), lambda h, n: (0, h)),
            scratch_shapes=[
                pltpu.VMEM((HD, SEQ), BF16),
                pltpu.VMEM((SEQ, HD), F32),
                pltpu.VMEM((SEQ, HD), F32),
            ],
        ),
        compiler_params=pltpu.CompilerParams(vmem_limit_bytes=56 << 20),
        cost_estimate=pl.CostEstimate(
            flops=340 * HINT * pairs, transcendentals=0, bytes_accessed=heads * SEQ * HD * 14
        ),
        name="attend_back",
    )(length, queries, key_rows, value_rows, grad, lse, *tables)


def hold(*values):
    return lax.optimization_barrier(values)


def swap_tensor(values, bit):
    count = lax.axis_size("tensor")
    return lax.ppermute(values, "tensor", [(t, t ^ bit) for t in range(count)])


def block_mask():
    return lax.axis_index("tensor") if lax.axis_size("tensor") == 4 else jnp.int32(0)


def near_blocks(block):
    if lax.axis_size("tensor") != 4:
        return [lax.all_gather(block, "tensor", axis=0, tiled=True)], None
    return [block, swap_tensor(block, 1)], swap_tensor(block, 2)


def far_blocks(far):
    return [far, swap_tensor(far, 1)]


def scatter_stages(sent, kept=None):
    if kept is None:
        (sent,) = yield (sent,)
        total = lax.psum_scatter(sent, "tensor", scatter_dimension=0, tiled=True)
        for _ in range(3):
            (total,) = yield (total,)
        return total.astype(F32)
    kept, sent = yield kept, sent
    kept, got = yield kept, swap_tensor(sent, 1)
    rows = kept.shape[0] // 2
    far = (kept[rows:].astype(F32) + got[rows:].astype(F32)).astype(BF16)
    far, kept, got = yield far, kept, got
    kept, got, mate = yield kept, got, swap_tensor(far, 2)
    return kept[:rows].astype(F32) + got[:rows].astype(F32) + mate.astype(F32)


def add_rows(left, right):
    return (left.astype(F32) + right.astype(F32)).astype(left.dtype)


def move_z(values, pairs):
    return lax.ppermute(values, "z", pairs)


INWARD = ((0, 1), (3, 2))
MIDDLE = ((1, 2), (2, 1))
OUTWARD = ((1, 0), (2, 3))


def on_edge():
    z = lax.axis_index("z")
    return (z == 0) | (z == 3)


def sum_line(values):
    values = add_rows(values, move_z(values, INWARD))
    values = add_rows(values, move_z(values, MIDDLE))
    return jnp.where(on_edge(), move_z(values, OUTWARD), values)


PAIRS = ((0, 1), (1, 0))


def line_stages(kept, sent):
    if lax.axis_size("z") != 4:
        for _ in range(10):
            kept, sent = yield kept, sent
        return lax.psum(kept, ("z", "y")), lax.psum(sent, ("z", "y"))
    kept, sent = yield kept, sent
    kept, got = yield kept, lax.ppermute(sent, "y", PAIRS)
    for pairs in (INWARD, MIDDLE):
        (kept,) = yield (add_rows(kept, got),)
        kept, got = yield kept, move_z(kept, pairs)
    (kept,) = yield (add_rows(kept, got),)
    kept, got = yield kept, move_z(kept, OUTWARD)
    (kept,) = yield (jnp.where(on_edge(), got, kept),)
    kept, got = yield kept, lax.ppermute(kept, "y", PAIRS)
    return kept, got


def own_half():
    return lax.axis_index("y") if lax.axis_size("z") == 4 else jnp.int32(0)


GATES = {
    "fc2_grad": ("+b",),
    "hidden_low": ("a", "+a"),
    "fc1_low": (),
    "hidden_high": ("+c",),
    "fc1_grad": ("b", "a", "+b", "+a"),
    "packed_low": ("+d",),
    "packed_high": ("c", "+c"),
    "attend_low": ("a", "+a"),
    "attend_high": ("b", "+b"),
    "dense_grad": ("d", "c", "a", "+e", "+a", "+d", "+c"),
    "back_low": ("b", "e", "+e", "+b"),
    "qkv_low": ("d", "c", "a", "+d", "+f"),
    "back_high": ("e", "b", "+e", "+c", "+b"),
    "qkv_high": ("d", "f", "+f", "+g"),
    "to_one": ("e", "c", "b", "+e", "+n1", "+c"),
    "to_two": ("f", "e", "g", "+f", "+g", "+d"),
    "to_out": ("n1", "+n2"),
}
TAIL = (
    ("f", "g", "c", "+e", "+n1", "+f"),
    ("d", "+g"),
    ("e", "+d"),
    ("n2", "+o"),
    ("f", "+n2"),
    ("g", "n1", "+g", "+f"),
    ("d",),
    ("o", "+o"),
    ("g", "n2", "+g"),
    ("f", "+s"),
    ("s", "+s"),
    ("o", "s", "+s"),
    ("g",),
    ("s", "+s"),
    ("s", "+s"),
    ("s", "+s"),
    ("s",),
)


class Piece:
    def __init__(self, stages):
        self.stages = stages
        self.waiting = next(stages)
        self.value = None
        self.fresh = True

    def step(self):
        try:
            self.waiting = self.stages.send(self.waiting)
        except StopIteration as end:
            self.value, self.waiting = end.value, ()


def hold_all(pieces, values):
    flat = list(values)
    for piece in pieces:
        flat.extend(piece.waiting)
    if not flat:
        return values
    flat = list(hold(*flat))
    start = len(values)
    for piece in pieces:
        end = start + len(piece.waiting)
        piece.waiting = tuple(flat[start:end])
        start = end
    return flat[: len(values)]


def gate(arrived, leaving, *values):
    values = hold_all(arrived, values)
    for piece in arrived:
        piece.step()
    values = hold_all([piece for piece in arrived if piece.waiting], values)
    for piece in leaving:
        piece.step()
    return values


def finish(*pieces):
    for piece in pieces:
        while piece.value is None:
            piece.step()
    return [piece.value for piece in pieces]


def small_stages(values):
    if lax.axis_size("z") != 4 or lax.axis_size("tensor") != 4:
        for _ in range(12):
            (values,) = yield (values,)
        return lax.psum(values, ("z", "y", "tensor"))
    moves = (
        lambda values: swap_tensor(values, 1),
        lambda values: swap_tensor(values, 2),
        lambda values: lax.ppermute(values, "y", PAIRS),
        lambda values: move_z(values, INWARD),
        lambda values: move_z(values, MIDDLE),
    )
    for move in moves:
        (values,) = yield (values,)
        values, got = yield values, move(values)
        values = values + got
    (values,) = yield (values,)
    values, got = yield values, move_z(values, OUTWARD)
    return jnp.where(on_edge(), got, values)


def gelu_parts(hidden):
    below = 0.5 * (1.0 + lax.erf(hidden * (0.5**0.5)))
    density = jnp.exp(-0.5 * hidden * hidden) * ((2.0 * jnp.pi) ** (-0.5))
    return hidden * below, below + hidden * density


def shards(
    inputs,
    lengths,
    ln1_gain,
    ln1_bias,
    ln2_gain,
    ln2_bias,
    w_qkv,
    b_qkv,
    w_dense,
    b_dense,
    w_fc1,
    b_fc1,
    w_fc2,
    b_fc2,
    out_grad,
):
    width = inputs.shape[1]
    tables = rotary_tables()
    scalars = jnp.stack([lengths[0], block_mask()])
    upper = own_half()
    half = width // 2
    near_in, far_in = near_blocks(inputs)
    near_low, far_low = near_blocks(out_grad[:, :half])
    near_high, far_high = near_blocks(out_grad[:, half:])
    vectors = [v.astype(F32)[None] for v in (ln1_gain, ln1_bias, ln2_gain, ln2_bias)]
    bias = b_fc1.astype(F32)[None]
    whole = SEQ
    split = far_in is not None
    parts = 2 if split else 1
    whole_one, whole_two = normalize(near_in, vectors, whole, 0)
    hidden, active = feed_forward(whole_two, w_fc1, bias, 0, parts)
    if far_in is not None:
        far_in, whole_one, whole_two, hidden, active = hold(
            far_in, whole_one, whole_two, hidden, active
        )
        whole_one, whole_two = normalize(
            far_blocks(far_in), vectors, whole, 1, (whole_one, whole_two)
        )
        hidden, active = feed_forward(whole_two, w_fc1, bias, 1, parts, (hidden, active))
        far_low, active = hold(far_low, active)
        near_low = near_low + far_blocks(far_low)
    grad_low = stack_rows(near_low)

    def half_gradient(left, right, side):
        rows = left.shape[1] // 2
        return dot_tn(lax.dynamic_slice_in_dim(left, side * rows, rows, 1), right).astype(BF16)

    def gradient(left, right):
        return hold(half_gradient(left, right, 1 - upper), left, right)

    def keep(left, right):
        return half_gradient(left, right, upper)

    token = scalars
    pieces = {}

    weights = {"a": "fc2", "b": "fc2", "c": "fc1", "d": "fc1", "e": "dense", "f": "qkv", "g": "qkv"}
    sums = {}

    def proceed(names, *values):
        ready = list(sums)
        came = [name for name in names if name[0] != "+"]
        leave = [pieces[name[1:]] for name in names if name[0] == "+"]
        arrived = [pieces[name] for name in came]
        values = hold_all([piece for piece in pieces.values() if piece.fresh], values)
        for piece in pieces.values():
            piece.fresh = False
        results = gate(arrived, leave, *values, *[sums[name] for name in ready])
        sums.update(zip(ready, results[len(values) :]))
        for name in came:
            weight = weights.get(name)
            if weight and pieces[name].value is not None:
                column = int(name in "bdg")
                sums[weight] = assemble(
                    pieces[name].value,
                    upper,
                    column,
                    1 if weight == "dense" else 2,
                    sums.get(weight),
                )
        return results[: len(values)]

    def at(place, *values):
        return proceed(GATES[place], *values)

    sent_a, active, grad_low = gradient(active, grad_low)
    kept_a = keep(active, grad_low)
    pieces["a"] = Piece(line_stages(kept_a, sent_a))
    pieces["a"].step()
    pieces["a"].fresh = False
    if far_high is not None:
        far_high, kept_a = hold(far_high, kept_a)
        near_high = near_high + far_blocks(far_high)
    grad_high = stack_rows(near_high)
    sent_b, kept_b = gradients(active, grad_high, upper)
    pieces["b"] = Piece(line_stages(kept_b, sent_b))
    grad_low, grad_high, kept_b, sent_b = at("fc2_grad", grad_low, grad_high, kept_b, sent_b)
    wide = w_fc2.shape[0] // 2

    def hidden_back(part, low, high):
        shape = (wide, half)
        return matmul(
            "nt",
            [(low, (w_fc2, shape, (part, 0))), (high, (w_fc2, shape, (part, 1)))],
            BF16,
            256,
            extras=[(hidden, part)],
            finish=lambda total, rows: total * gelu_parts(rows)[1],
            chunk=512,
            name="hidden_grad",
        )

    hidden_low = hidden_back(0, grad_low, grad_high)
    hidden_low, whole_two, grad_low = at("hidden_low", hidden_low, whole_two, grad_low)
    sent_c, kept_c = gradients(whole_two, hidden_low, upper)
    pieces["c"] = Piece(line_stages(kept_c, sent_c))
    kept_c, sent_c, grad_low = at("fc1_low", kept_c, sent_c, grad_low)
    hidden_high = hidden_back(1, grad_low, grad_high)
    hidden_high, whole_two = at("hidden_high", hidden_high, whole_two)
    sent_d, kept_d = gradients(whole_two, hidden_high, upper)
    fc1_bias_grad = jnp.concatenate(
        [jnp.sum(part, axis=0, dtype=F32) for part in (hidden_low, hidden_high)]
    )
    pieces["d"] = Piece(line_stages(kept_d, sent_d))
    kept_d, sent_d, whole_one = at("fc1_grad", kept_d, sent_d, whole_one)

    columns = w_qkv.shape[1] // 2

    def project(part, rows):
        return matmul(
            "nn",
            [(rows, (w_qkv, (width, columns), (0, part)))],
            F32,
            512,
            extras=[b_qkv[part * columns : (part + 1) * columns].astype(F32)[None]],
            finish=jnp.add,
            name="packed",
        )

    packed_low = project(0, whole_one)
    packed_low, whole_one = at("packed_low", packed_low, whole_one)
    packed_high = project(1, whole_one)
    packed_low, packed_high = at("packed_high", packed_low, packed_high)
    saved_low = attend(packed_low, scalars, tables)
    packed_high, *saved_low = at("attend_low", packed_high, *saved_low)
    saved_high = attend(packed_high, scalars, tables)
    context = jnp.concatenate([saved_low[3], saved_high[3]], axis=1)
    context, grad_low = at("attend_high", context, grad_low)
    sent_low, kept_low = gradients(context, grad_low, upper)
    sent_high, kept_high = gradients(context, grad_high, upper)
    sent_e = jnp.concatenate([sent_low, sent_high], axis=1)
    kept_e = jnp.concatenate([kept_low, kept_high], axis=1)
    inner = w_dense.shape[0] // 2
    pieces["e"] = Piece(line_stages(kept_e, sent_e))
    grad_low, kept_e, sent_e = at("dense_grad", grad_low, kept_e, sent_e)

    def back(part, saved, low):
        shape = (inner, half)
        grad = matmul(
            "nt",
            [(low, (w_dense, shape, (part, 0))), (grad_high, (w_dense, shape, (part, 1)))],
            BF16,
            512,
            name="context_grad",
        )
        queries, key_rows, value_rows, _, lse = saved
        return attend_back(queries, key_rows, value_rows, grad, lse, scalars, tables)

    back_low = back(0, saved_low, grad_low)
    back_low, grad_low, whole_one = at("back_low", back_low, grad_low, whole_one)
    sent_f, kept_f = gradients(whole_one, back_low, upper)
    pieces["f"] = Piece(line_stages(kept_f, sent_f))
    kept_f, sent_f, grad_low = at("qkv_low", kept_f, sent_f, grad_low)
    back_high = back(1, saved_high, grad_low)
    back_high, whole_one = at("back_high", back_high, whole_one)
    sent_g, kept_g = gradients(whole_one, back_high, upper)
    packed_grad = jnp.concatenate([back_low, back_high], axis=1)
    qkv_bias_grad = jnp.sum(packed_grad, axis=0, dtype=F32)
    pieces["g"] = Piece(line_stages(kept_g, sent_g))
    packed_grad, kept_g, sent_g = at("qkv_high", packed_grad, kept_g, sent_g)
    to_one = matmul("nt", [(packed_grad, w_qkv)], BF16, 512, split=split, name="to_one")
    pieces["n1"] = Piece(scatter_stages(*to_one) if split else scatter_stages(to_one))
    (hidden_low,) = at("to_one", hidden_low)
    to_two = matmul(
        "nt",
        [
            (hidden_low, (w_fc1, (width, wide), (0, 0))),
            (hidden_high, (w_fc1, (width, wide), (0, 1))),
        ],
        BF16,
        512,
        split=split,
        name="to_two",
    )
    pieces["n2"] = Piece(scatter_stages(*to_two) if split else scatter_stages(to_two))
    context, active = at("to_two", context, active)
    to_out = matmul(
        "nn", [(context, w_dense), (active, w_fc2)], BF16, 512, split=split, name="to_out"
    )
    pieces["o"] = Piece(scatter_stages(*to_out) if split else scatter_stages(to_out))
    (token,) = at("to_out", token)

    own_rows = inputs.astype(F32)
    own_grad = out_grad.astype(F32)

    def norms_back(normed_one, normed_two):
        middle = own_rows - jnp.mean(own_rows, axis=-1, keepdims=True)
        spread = jnp.mean(middle * middle, axis=-1, keepdims=True)
        rate = lax.rsqrt(spread + EPS)
        own_hat = middle * rate

        def norm_back(grad, gain):
            scaled = grad * gain.astype(F32)
            return rate * (
                scaled
                - jnp.mean(scaled, axis=-1, keepdims=True)
                - own_hat * jnp.mean(scaled * own_hat, axis=-1, keepdims=True)
            )

        in_grad = own_grad + norm_back(normed_one, ln1_gain) + norm_back(normed_two, ln2_gain)
        shared = jnp.stack(
            [
                jnp.sum(normed_one * own_hat, axis=0),
                jnp.sum(normed_one, axis=0),
                jnp.sum(normed_two * own_hat, axis=0),
                jnp.sum(normed_two, axis=0),
                jnp.sum(own_grad, axis=0),
            ]
        )
        return in_grad, shared

    sliced = jnp.concatenate([qkv_bias_grad, fc1_bias_grad])
    place = lax.axis_index("tensor")
    slots = jnp.zeros((lax.axis_size("tensor"), sliced.shape[0]), F32)
    slots = lax.dynamic_update_slice_in_dim(slots, sliced[None], place, 0)
    common = 5 * width
    for names in TAIL:
        (token,) = proceed(names, token)
        if "s" not in pieces and None not in (pieces["n1"].value, pieces["n2"].value):
            in_grad, shared = norms_back(pieces["n1"].value, pieces["n2"].value)
            small = jnp.concatenate([shared.reshape(-1), slots.reshape(-1)]).reshape(-1, HD)
            pieces["s"] = Piece(small_stages(small))
    branches, total = finish(pieces["o"], pieces["s"])
    total = total.reshape(-1)
    vectors = total[:common].reshape(5, width)
    slots = total[common:].reshape(slots.shape)
    own_slot = lax.dynamic_index_in_dim(slots, place, 0, False)
    outputs = own_rows + branches + (b_dense.astype(F32) + b_fc2.astype(F32))
    return (
        outputs.astype(BF16),
        in_grad,
        vectors[0],
        vectors[1],
        vectors[2],
        vectors[3],
        sums["qkv"],
        own_slot[: b_qkv.shape[0]],
        sums["dense"],
        vectors[4],
        sums["fc1"],
        own_slot[b_qkv.shape[0] :],
        sums["fc2"],
        vectors[4],
    )


def solution(mesh):
    sequences, width = mesh.shape["dp"], mesh.shape["tensor"]
    mesh = Mesh(mesh.devices.reshape(sequences // 2, 2, width), ("z", "y", "tensor"))
    rows = P(("z", "y", "tensor"), None)
    columns = P(None, "tensor")
    inner = P("tensor", None)
    split = P("tensor")
    return jax.shard_map(
        shards,
        mesh=mesh,
        in_specs=(
            rows,
            P(("z", "y")),
            P(),
            P(),
            P(),
            P(),
            columns,
            split,
            inner,
            P(),
            columns,
            split,
            inner,
            P(),
            rows,
        ),
        out_specs=(
            rows,
            rows,
            P(),
            P(),
            P(),
            P(),
            columns,
            split,
            inner,
            P(),
            columns,
            split,
            inner,
            P(),
        ),
        check_vma=False,
    )
```
